32 devices in a mesh: band: 8 (over z, x), cuts: 4 (over y, core).
Axes of the slice: x: 2, y: 2, z: 4, core: 2. Of those that a mesh axis runs over, the one named last changes fastest.
Arguments:
- var_feat: bfloat16 [163840, 128], P(('band', 'cuts')), may hold values from -6 to 6
- con_feat: bfloat16 [4096, 128], P(('band', 'cuts')), may hold values from -6 to 6
- slot_column_block: int32 [5120], P(('band', 'cuts')), may hold values from 0 to 39
- slot_constraint_block: int32 [5120], P(('band', 'cuts')), may hold values from 0 to 7
- block_count: int32 [32], P(('band', 'cuts')), may hold values from 40 to 160, as said below
- incidence_coefficients: int32 [5120, 128, 128], P(('band', 'cuts')), may hold values from -3 to 4
- con_first: bfloat16 [256, 256], replicated, may hold values from -0.375 to 0.375
- con_bias: float32 [256], replicated, may hold values from -3 to 3
- con_second: bfloat16 [256, 256], replicated, may hold values from -0.375 to 0.375
- con_third: bfloat16 [256, 128], replicated, may hold values from -0.375 to 0.375
- con_gain: float32 [128], replicated, may hold values from 0.1 to 1.9
- con_shift: float32 [128], replicated, may hold values from -3 to 3
- var_first: bfloat16 [256, 256], replicated, may hold values from -0.375 to 0.375
- var_bias: float32 [256], replicated, may hold values from -3 to 3
- var_second: bfloat16 [256, 256], replicated, may hold values from -0.375 to 0.375
- var_third: bfloat16 [256, 128], replicated, may hold values from -0.375 to 0.375
- var_gain: float32 [128], replicated, may hold values from 0.1 to 1.9
- var_shift: float32 [128], replicated, may hold values from -3 to 3
Outputs:
- con_new: bfloat16 [4096, 128], P(('band', 'cuts'))
- var_new: bfloat16 [163840, 128], P(('band', 'cuts'))
The draws below stay inside these ranges and needn't reach their ends.
Inputs may be any that keep to these rules, and one draw needn't show every extreme that they name: Each device's live slots are its first block_count slots; in every draw one eighth of the devices hold 160 live slots and some device holds 40.
All inputs are finite; a program needn't handle non-finite values.
Results may differ from the reference program's by a relative error of at most 0.0075.
Values may be sent and summed in bfloat16 or wider, within the bound.
A program may use at most 128 MiB of HBM per device.

```python
import math
import jax
import jax.numpy as jnp
from jax import lax

W = 128
HID = 256
INCIDENCE_ORDER = 128
CONSTRAINT_BLKS = 1
PATTERN_BLOCKS = 40
NB = 160
NV = 163840
NC = 4096
TOTAL_SLOTS = 5120
N_BAND = 8
N_CUTS = 4


def draw_block_count(key, part):
    device_total = N_BAND * N_CUTS
    first_key, second_key = jax.random.split(key)
    live_slots = PATTERN_BLOCKS + jax.random.randint(first_key, (device_total,), 0, PATTERN_BLOCKS + 1)
    shuffled = jax.random.permutation(second_key, device_total)
    full_rank = jnp.zeros((device_total,), jnp.int32).at[shuffled].set(jnp.arange(device_total, dtype=jnp.int32))
    heavy = full_rank < device_total // 8
    live_slots = jnp.where(heavy, 4 * PATTERN_BLOCKS, live_slots)
    live_slots = jnp.where(full_rank == device_total - 1, PATTERN_BLOCKS, live_slots)
    return live_slots.astype(jnp.int32)


def plant(result, key, least, top_value):
    shape = result.shape
    spot = [jax.random.randint(jax.random.fold_in(key, axis), (), 0, shape[axis]) for axis in range(len(shape))]
    result = result.at[tuple(spot)].set(least)
    longest = shape.index(max(shape))
    spot[longest] = (spot[longest] + 1) % shape[longest]
    return result.at[tuple(spot)].set(top_value)


def levels(rng, extent, cuts, low, largest):
    level = 1.0
    for axis_at, parts in cuts:
        heights = jax.random.uniform(jax.random.fold_in(jax.random.fold_in(rng, 6), axis_at), (parts,), jnp.float32, low / len(cuts), largest / len(cuts))
        level = level * jnp.repeat(jnp.exp(heights), extent[axis_at] // parts).reshape((-1,) + (1,) * (len(extent) - 1 - axis_at))
    return level


def scatter_about(rng, extent, scale, bound, shards=(), kind=jnp.bfloat16):
    entries = scale * jax.random.normal(rng, extent, jnp.float32)
    if shards:
        entries = entries * levels(rng, extent, shards, -0.22, 0.18)
    return jnp.clip(entries, -bound, bound).astype(kind)


def setup_inputs(seed: int = 0) -> dict:
    seeds = jax.random.split(jax.random.key(seed), 19)
    var_feat = scatter_about(seeds[0], (NV, W), 1.0, 6.0, ((0, 32),))
    con_feat = scatter_about(seeds[1], (NC, W), 1.0, 6.0, ((0, 32),))
    slot_column_block = plant(jax.random.randint(seeds[2], (TOTAL_SLOTS,), 0, PATTERN_BLOCKS), jax.random.fold_in(seeds[2], 1), 0, PATTERN_BLOCKS - 1).astype(jnp.int32)
    slot_constraint_block = plant(jax.random.randint(seeds[3], (TOTAL_SLOTS,), 0, 2 * CONSTRAINT_BLKS * N_CUTS), jax.random.fold_in(seeds[3], 1), 0, (2 * CONSTRAINT_BLKS * N_CUTS) - 1).astype(jnp.int32)
    block_count = draw_block_count(jax.random.fold_in(seeds[18], 71), 0)
    incidence_coefficients = plant(jax.random.randint(seeds[5], (TOTAL_SLOTS, INCIDENCE_ORDER, INCIDENCE_ORDER), -3, 5), jax.random.fold_in(seeds[5], 1), -3, 4).astype(jnp.int32)
    con_first = scatter_about(seeds[6], (2 * W, HID), (2 * W) ** -0.5, 0.375)
    con_bias = scatter_about(seeds[7], (HID,), 0.5, 3.0, (), jnp.float32)
    con_second = scatter_about(seeds[8], (HID, HID), HID ** -0.5, 0.375)
    con_third = scatter_about(seeds[9], (HID, W), HID ** -0.5, 0.375)
    con_gain = jnp.clip(1.0 + 0.18 * jax.random.normal(seeds[10], (W,), jnp.float32), 0.1, 1.9)
    con_shift = scatter_about(seeds[11], (W,), 0.5, 3.0, (), jnp.float32)
    var_first = scatter_about(seeds[12], (2 * W, HID), (2 * W) ** -0.5, 0.375)
    var_bias = scatter_about(seeds[13], (HID,), 0.5, 3.0, (), jnp.float32)
    var_second = scatter_about(seeds[14], (HID, HID), HID ** -0.5, 0.375)
    var_third = scatter_about(seeds[15], (HID, W), HID ** -0.5, 0.375)
    var_gain = jnp.clip(1.0 + 0.18 * jax.random.normal(seeds[16], (W,), jnp.float32), 0.1, 1.9)
    var_shift = scatter_about(seeds[17], (W,), 0.5, 3.0, (), jnp.float32)
    return {"var_feat": var_feat, "con_feat": con_feat, "slot_column_block": slot_column_block, "slot_constraint_block": slot_constraint_block, "block_count": block_count, "incidence_coefficients": incidence_coefficients, "con_first": con_first, "con_bias": con_bias, "con_second": con_second, "con_third": con_third, "con_gain": con_gain, "con_shift": con_shift, "var_first": var_first, "var_bias": var_bias, "var_second": var_second, "var_third": var_third, "var_gain": var_gain, "var_shift": var_shift}


EPS = 1e-05

def layer_norm(values, gain, offset):
    center = values - lax.optimization_barrier(jnp.mean(values, axis=-1, keepdims=True))
    spread = lax.optimization_barrier(jnp.mean(center * center, axis=-1, keepdims=True))
    return center * lax.rsqrt(spread + EPS) * gain + offset

def node_update(feats, scaled_agg, w_first, bias, w_second, w_third, gain, offset):
    joined = jnp.concatenate([feats, scaled_agg.astype(jnp.bfloat16)], axis=1)
    hidden = jnp.maximum(jnp.dot(joined, w_first, preferred_element_type=jnp.float32) + bias, 0.0).astype(jnp.bfloat16)
    middle = jnp.maximum(jnp.dot(hidden, w_second, preferred_element_type=jnp.float32), 0.0).astype(jnp.bfloat16)
    output = jnp.dot(middle, w_third, preferred_element_type=jnp.float32)
    return layer_norm(feats.astype(jnp.float32) + output, gain, offset).astype(jnp.bfloat16)

def reference(var_feat, con_feat, slot_column_block, slot_constraint_block, block_count, incidence_coefficients, con_first, con_bias, con_second, con_third, con_gain, con_shift, var_first, var_bias, var_second, var_third, var_gain, var_shift):
    device_total = N_BAND * N_CUTS
    band_blocks = CONSTRAINT_BLKS * N_CUTS
    band_rows = band_blocks * INCIDENCE_ORDER
    width = var_feat.shape[1]
    var_blocks = var_feat.reshape(device_total, PATTERN_BLOCKS, INCIDENCE_ORDER, width)
    col_index = slot_column_block.reshape(device_total, NB)
    row_index = slot_constraint_block.reshape(device_total, NB)
    coef_all = incidence_coefficients.reshape(device_total, NB, INCIDENCE_ORDER, INCIDENCE_ORDER)
    slot_ids = jnp.arange(NB, dtype=jnp.int32)
    row_ids = jnp.arange(2 * band_blocks, dtype=jnp.int32)
    col_ids = jnp.arange(PATTERN_BLOCKS, dtype=jnp.int32)
    highest = lax.Precision.HIGHEST

    def accumulate(carry, device):
        live = (slot_ids < block_count[device]).astype(jnp.float32)
        picked = jnp.take(var_blocks[device], col_index[device], axis=0).astype(jnp.float32)
        coef = coef_all[device].astype(jnp.float32)
        products = jnp.einsum('sij,sjw->siw', coef, picked, precision=highest)
        selector = (row_index[device][None, :] == row_ids[:, None]).astype(jnp.float32) * live[None, :]
        term = jnp.einsum('rs,siw->riw', selector, products, precision=highest).reshape(2 * band_rows, width)
        start = device // N_CUTS * band_rows
        current = lax.dynamic_slice_in_dim(carry, start, 2 * band_rows, 0)
        return (lax.dynamic_update_slice_in_dim(carry, current + term, start, 0), None)
    padded = jnp.zeros((NC + band_rows, width), jnp.float32)
    con_agg, _ = lax.scan(accumulate, padded, jnp.arange(device_total, dtype=jnp.int32))
    con_agg = con_agg[:NC] * (1.0 / math.sqrt(INCIDENCE_ORDER * NB))
    con_new = node_update(con_feat, con_agg, con_first, con_bias, con_second, con_third, con_gain, con_shift)
    con_padded = jnp.concatenate([con_new, jnp.zeros((band_rows, width), jnp.bfloat16)], axis=0)

    def update(device):
        live = (slot_ids < block_count[device]).astype(jnp.float32)
        start = device // N_CUTS * band_rows
        window = lax.dynamic_slice_in_dim(con_padded, start, 2 * band_rows, 0).reshape(2 * band_blocks, INCIDENCE_ORDER, width)
        picked = jnp.take(window, row_index[device], axis=0).astype(jnp.float32)
        coef = coef_all[device].astype(jnp.float32)
        products = jnp.einsum('sij,siw->sjw', coef, picked, precision=highest)
        selector = (col_index[device][None, :] == col_ids[:, None]).astype(jnp.float32) * live[None, :]
        var_agg = jnp.einsum('cs,sjw->cjw', selector, products, precision=highest).reshape(PATTERN_BLOCKS * INCIDENCE_ORDER, width)
        var_agg = var_agg * (1.0 / math.sqrt(4 * INCIDENCE_ORDER))
        own_feat = var_blocks[device].reshape(PATTERN_BLOCKS * INCIDENCE_ORDER, width)
        return node_update(own_feat, var_agg, var_first, var_bias, var_second, var_third, var_gain, var_shift)
    var_new = lax.map(update, jnp.arange(device_total, dtype=jnp.int32)).reshape(NV, width)
    return (con_new, var_new)
```

```python
import functools
import math

import jax
import jax.numpy as jnp
from jax import lax
from jax.experimental import pallas as pl
from jax.experimental.pallas import tpu as pltpu
from jax.sharding import PartitionSpec as P

EPS = 1e-05
F32 = jnp.float32
BF16 = jnp.bfloat16
FP8 = jnp.float8_e4m3fn
MESH = pl.DeviceIdType.MESH
CHUNK = 16
UNROLL = 8
FORWARD = 22
BACK = 25
PAIR = 5
GATHER = 8
TILE = 512
FEAT_SCALE = 64.0
CON_SCALE = 16.0
LOW_SCALE = 16.0


def layer_norm(values, gain, offset):
    center = values - jnp.mean(values, axis=-1, keepdims=True)
    spread = jnp.mean(center * center, axis=-1, keepdims=True)
    return center * lax.rsqrt(spread + EPS) * gain + offset


def node_update(feats, scaled_agg, w_first, bias, w_second, w_third, gain, offset):
    joined = jnp.concatenate([feats, scaled_agg.astype(BF16)], axis=1)
    hidden = jnp.maximum(jnp.dot(joined, w_first, preferred_element_type=F32) + bias, 0.0).astype(BF16)
    middle = jnp.maximum(jnp.dot(hidden, w_second, preferred_element_type=F32), 0.0).astype(BF16)
    output = jnp.dot(middle, w_third, preferred_element_type=F32)
    return layer_norm(feats.astype(F32) + output, gain, offset).astype(BF16)


def split(values, scale):
    scaled = values.astype(F32) * scale
    high = scaled.astype(FP8)
    low = ((scaled - high.astype(F32)) * LOW_SCALE).astype(FP8)
    return high, low


def join(products, width):
    return products[:, :width] + products[:, width:] * (1.0 / LOW_SCALE)


def order_rows(key_row, key_col, other_col, live_row, live_col, lanes, low, start):
    slots = key_col.shape[0]
    iota = lambda shape, axis: lax.broadcasted_iota(jnp.int32, shape, axis)
    lane = iota((slots, lanes), 1)
    before = (key_row == key_col) & (iota((slots, slots), 1) < iota((slots, slots), 0))
    within = jnp.sum(jnp.where(before, live_row, 0), axis=1, keepdims=True)
    counts = jnp.sum(jnp.where(lane == key_col, live_col, 0), axis=0, keepdims=True)
    counts_col = jnp.sum(jnp.where(iota((lanes, slots), 0) == key_row, live_row, 0), axis=1, keepdims=True)
    steps, steps_col = (counts + 1) >> 1, (counts_col + 1) >> 1
    floor = jnp.where(key_col >= low, low, 0)
    chosen = (lane < key_col) & (lane >= floor)
    base_col = jnp.sum(jnp.where(chosen, steps, 0), axis=1, keepdims=True) + jnp.where(key_col >= low, start, 0)
    place = jnp.where(live_col > 0, base_col * 2 + within, -1)
    hit = place == lane
    index = jnp.sum(jnp.where(hit, iota((slots, lanes), 0) - slots, 0), axis=0, keepdims=True) + slots
    other = jnp.sum(jnp.where(hit, other_col, 0), axis=0, keepdims=True)
    opens = (place == lane * 2) & (within == 0)
    carry = 1 - jnp.sum(jnp.where(opens, 1, 0), axis=0, keepdims=True)
    above, below = iota((lanes, lanes), 0), iota((lanes, lanes), 1)
    upto = (above <= below) & ((above >= low) == (below >= low))
    ends = jnp.sum(jnp.where(upto, steps_col, 0), axis=0, keepdims=True)
    ends += jnp.where(iota((1, lanes), 1) >= low, start, 0)
    last = jnp.maximum(ends - 1, 0)
    filled = jnp.where(counts > 0, 1, 0)
    rows = [index, other, carry, last, filled]
    return jnp.concatenate(rows + [jnp.zeros((1, lanes), jnp.int32)] * (8 - len(rows)), axis=0)


def kernel(
    dims,
    cb_hbm, rb_hbm, count_s, vf_hbm, cf_hbm, coef_hbm, *refs,
):
    nb, nc, slots, size, cols, fpairs, pairs, lanes, chunks = dims
    con_weights_hbm, var_weights_hbm, refs = refs[:6], refs[6:12], refs[12:]
    con_out, agg_out, feat, refs = refs[0], refs[1], refs[2], refs[3:]
    var_weights, refs = refs[:6], refs[6:]
    cb_v, rb_v, cf, con_weights, refs = refs[0], refs[1], refs[2], refs[3:9], refs[9:]
    (
        raw, half, scan, paired, feat8, part, arrive, window, win8, conbuf,
        orderf_v, orderf_s, orderb_v, orderb_s,
        raw_sem, feat_sem, small_sem, weight_sem, order_sem, psend, precv, wsend, wrecv,
    ) = refs
    band = lax.axis_index("band")
    cut = lax.axis_index("cuts")
    has_next = band < nb - 1
    has_prev = band > 0
    width = feat.shape[1]

    small = [
        pltpu.make_async_copy(src, dst, small_sem.at[i])
        for i, (src, dst) in enumerate(((cb_hbm, cb_v), (rb_hbm, rb_v)))
    ]
    for copy in small:
        copy.start()

    def raw_copy(i):
        piece = pl.ds(i * CHUNK, CHUNK)
        return pltpu.make_async_copy(coef_hbm.at[piece], raw.at[piece], raw_sem.at[i])

    for i in range(chunks // 2):
        raw_copy(i).start()
    feat_copy = pltpu.make_async_copy(vf_hbm, feat, feat_sem)
    feat_copy.start()
    for i in range(chunks // 2, chunks):
        raw_copy(i).start()
    weights = [
        pltpu.make_async_copy(src, dst, weight_sem.at[i])
        for i, (src, dst) in enumerate(
            zip((cf_hbm, *con_weights_hbm, *var_weights_hbm), (cf, *con_weights, *var_weights)))
    ]
    for copy in weights:
        copy.start()

    barrier = pltpu.get_barrier_semaphore()
    for d in range(1, nc):
        pl.semaphore_signal(barrier, inc=1, device_id=(band, lax.rem(cut + d, nc)), device_id_type=MESH)

    @pl.when(has_next)
    def _():
        for d in range(nc):
            pl.semaphore_signal(barrier, inc=1, device_id=(band + 1, lax.rem(cut + d, nc)), device_id_type=MESH)

    @pl.when(has_prev)
    def _():
        for d in range(nc):
            pl.semaphore_signal(barrier, inc=1, device_id=(band - 1, lax.rem(cut + d, nc)), device_id_type=MESH)

    half[slots] = jnp.zeros((size, size), FP8)

    @pl.when(jnp.logical_not(has_prev))
    def _():
        arrive[pl.ds(nc, nc)] = jnp.zeros((nc,) + arrive.shape[1:], BF16)

    @pl.when(jnp.logical_not(has_next))
    def _():
        window[pl.ds(nc, nc)] = jnp.zeros((nc,) + window.shape[1:], BF16)

    for copy in small:
        copy.wait()
    row_c = cb_v[...]
    row_r = rb_v[...]
    diagonal = lax.broadcasted_iota(jnp.int32, (slots, slots), 0) == lax.broadcasted_iota(jnp.int32, (slots, slots), 1)
    col_c = jnp.sum(jnp.where(diagonal, row_c, 0), axis=1, keepdims=True)
    col_r = jnp.sum(jnp.where(diagonal, row_r, 0), axis=1, keepdims=True)
    count = count_s[0]
    early = chunks // 2 * CHUNK
    live_row = jnp.where(lax.broadcasted_iota(jnp.int32, (1, slots), 1) < count, 1, 0)
    live_col = jnp.where(lax.broadcasted_iota(jnp.int32, (slots, 1), 0) < count, 1, 0)
    blocks = part.shape[1] // size
    keys = 2 * nc * blocks
    late_row = jnp.where(lax.broadcasted_iota(jnp.int32, (1, slots), 1) >= early, keys, 0)
    late_col = jnp.where(lax.broadcasted_iota(jnp.int32, (slots, 1), 0) >= early, keys, 0)
    orderf_v[...] = order_rows(row_r + late_row, col_r + late_col, col_c, live_row, live_col, lanes, keys, fpairs // 2)
    orderf_copy = pltpu.make_async_copy(orderf_v, orderf_s, order_sem.at[0])
    orderf_copy.start()

    def convert(i, _):
        raw_copy(i).wait()

        def some(j, _):
            for u in range(UNROLL):
                at = i * CHUNK + j * UNROLL + u
                half[at] = raw[at].astype(F32).astype(FP8)
            return 0

        lax.fori_loop(0, CHUNK // UNROLL, some, 0)
        return 0

    lax.fori_loop(0, chunks // 2, convert, 0)
    feat_copy.wait()

    def split_feat(i, _):
        for u in range(GATHER // 2):
            at = i * (GATHER // 2) + u
            high, low = split(feat[pl.ds(pl.multiple_of(at * size, size), size)], FEAT_SCALE)
            feat8[at, :, :width] = high
            feat8[at, :, width:] = low
        return 0

    lax.fori_loop(0, cols // (GATHER // 2), split_feat, 0)
    orderf_copy.wait()

    def forward(k, carry):
        for u in range(FORWARD):
            at = k * FORWARD + u
            left = jnp.concatenate([half[orderf_s[0, 2 * at]], half[orderf_s[0, 2 * at + 1]]], axis=1)
            right = jnp.concatenate([feat8[orderf_s[1, 2 * at]], feat8[orderf_s[1, 2 * at + 1]]], axis=0)
            term = join(jnp.dot(left, right, preferred_element_type=F32), width)
            carry = carry * orderf_s[2, at].astype(F32) + term
            scan[at] = carry
        return carry

    turns = fpairs // FORWARD
    carry = lax.fori_loop(0, turns // 2, forward, jnp.zeros(scan.shape[1:], F32))
    lax.fori_loop(chunks // 2, chunks, convert, 0)
    lax.fori_loop(turns // 2, turns, forward, carry)

    def fill(q):
        for e in range(blocks):
            r = q * blocks + e
            sums = scan[orderf_s[3, r]] * orderf_s[4, r].astype(F32)
            sums += scan[orderf_s[3, keys + r]] * orderf_s[4, keys + r].astype(F32)
            part[q, e * size : (e + 1) * size] = (sums * (1.0 / FEAT_SCALE)).astype(BF16)

    def part_send(d, ahead):
        to = lax.rem(cut + d, nc)
        q = ahead * nc + d
        return pltpu.make_async_remote_copy(
            src_ref=part.at[ahead * nc + to], dst_ref=arrive.at[ahead * nc + cut],
            send_sem=psend.at[q], recv_sem=precv.at[ahead * nc + cut],
            device_id=(band + ahead, to), device_id_type=MESH)

    def part_wait(src, ahead):
        pltpu.make_async_remote_copy(
            src_ref=part.at[0], dst_ref=arrive.at[ahead * nc + src],
            send_sem=psend.at[0], recv_sem=precv.at[ahead * nc + src],
            device_id=(band, cut), device_id_type=MESH).wait_recv()

    for q in range(2 * nc):
        fill(q)

    expected = (nc - 1) + jnp.where(has_next, nc, 0) + jnp.where(has_prev, nc, 0)
    pl.semaphore_wait(barrier, expected)

    @pl.when(has_next)
    def _():
        for d in range(nc):
            part_send(d, 1).start()

    for d in range(1, nc):
        part_send(d, 0).start()

    orderb_v[...] = order_rows(row_c, col_c, col_r, live_row, live_col, lanes, lanes, 0)
    orderb_copy = pltpu.make_async_copy(orderb_v, orderb_s, order_sem.at[1])
    orderb_copy.start()
    for copy in weights:
        copy.wait()
    orderb_copy.wait()

    def pair_up(p, _):
        for u in range(PAIR):
            k = p * PAIR + u
            paired[k, :, :size] = half[orderb_s[0, 2 * k]].T
            paired[k, :, size:] = half[orderb_s[0, 2 * k + 1]].T
        return 0

    lax.fori_loop(0, pairs // PAIR, pair_up, 0)

    total = part[cut].astype(F32)
    for d in range(1, nc):
        src = lax.rem(cut + d, nc)
        part_wait(src, 0)
        total += arrive[src].astype(F32)

    @pl.when(has_prev)
    def _():
        for src in range(nc):
            part_wait(src, 1)

    for src in range(nc):
        total += arrive[nc + src].astype(F32)

    con_new = node_update(cf[...], total * (1.0 / math.sqrt(size * slots)), *(w[...] for w in con_weights))
    conbuf[...] = con_new
    window[cut] = con_new

    def win_send(d, back):
        to = lax.rem(cut + d, nc)
        return pltpu.make_async_remote_copy(
            src_ref=conbuf, dst_ref=window.at[back * nc + cut],
            send_sem=wsend.at[back * nc + d], recv_sem=wrecv.at[back * nc + cut],
            device_id=(band - back, to), device_id_type=MESH)

    def win_wait(src, back):
        pltpu.make_async_remote_copy(
            src_ref=conbuf, dst_ref=window.at[back * nc + src],
            send_sem=wsend.at[0], recv_sem=wrecv.at[back * nc + src],
            device_id=(band, cut), device_id_type=MESH).wait_recv()

    @pl.when(has_prev)
    def _():
        for d in range(nc):
            win_send(d, 1).start()

    for d in range(1, nc):
        win_send(d, 0).start()

    con_out[...] = con_new

    @pl.when(has_next)
    def _():
        for d in range(nc):
            part_send(d, 1).wait_send()

    for d in range(1, nc):
        part_send(d, 0).wait_send()

    def split_con(q):
        for e in range(blocks):
            high, low = split(window[q, e * size : (e + 1) * size], CON_SCALE)
            win8[q * blocks + e, :, :width] = high
            win8[q * blocks + e, :, width:] = low

    for d in range(1, nc):
        win_wait(lax.rem(cut + d, nc), 0)
    for q in range(nc):
        split_con(q)

    @pl.when(has_next)
    def _():
        for src in range(nc):
            win_wait(src, 1)

    for q in range(nc, 2 * nc):
        split_con(q)

    def back(k, carry):
        for u in range(BACK):
            at = k * BACK + u
            right = jnp.concatenate([win8[orderb_s[1, 2 * at]], win8[orderb_s[1, 2 * at + 1]]], axis=0)
            term = join(jnp.dot(paired[at], right, preferred_element_type=F32), width)
            carry = carry * orderb_s[2, at].astype(F32) + term
            scan[at] = carry
        return carry

    lax.fori_loop(0, pairs // BACK, back, jnp.zeros(scan.shape[1:], F32))

    scale = 1.0 / (CON_SCALE * math.sqrt(4 * size))

    def gather(i, _):
        for u in range(GATHER):
            c = i * GATHER + u
            sums = scan[orderb_s[3, c]] * (orderb_s[4, c].astype(F32) * scale)
            agg_out[pl.ds(pl.multiple_of(c * size, size), size)] = sums.astype(BF16)
        return 0

    lax.fori_loop(0, cols // GATHER, gather, 0)

    @pl.when(has_prev)
    def _():
        for d in range(nc):
            win_send(d, 1).wait_send()

    for d in range(1, nc):
        win_send(d, 0).wait_send()


def column_kernel(
    feat, agg, con, vw1, vbias, vw2, vw3, vgain, vshift, con_out, var_out,
    result, hidden, middle, output, out_sem, con_sem,
):
    con_copy = pltpu.make_async_copy(con, con_out, con_sem)
    con_copy.start()
    tiles = feat.shape[0] // TILE
    piece = lambda i: pl.ds(i * TILE, TILE)

    def out_copy(i):
        return pltpu.make_async_copy(result.at[piece(i)], var_out.at[piece(i)], out_sem.at[i])

    def first(i):
        joined = jnp.concatenate([feat[piece(i)], agg[piece(i)]], axis=1)
        sums = jnp.dot(joined, vw1[...], preferred_element_type=F32) + vbias[...]
        hidden[i % 2] = jnp.maximum(sums, 0.0).astype(BF16)

    def second(i):
        sums = jnp.dot(hidden[i % 2], vw2[...], preferred_element_type=F32)
        middle[i % 2] = jnp.maximum(sums, 0.0).astype(BF16)

    def third(i):
        sums = jnp.dot(middle[i % 2], vw3[...], preferred_element_type=F32)
        output[i % 2] = feat[piece(i)].astype(F32) + sums

    def norm(i):
        result[piece(i)] = layer_norm(output[i % 2], vgain[...], vshift[...]).astype(BF16)
        out_copy(i).start()

    stages = (norm, 3), (third, 2), (second, 1), (first, 0)
    for t in range(tiles + len(stages) - 1):
        for stage, delay in stages:
            if 0 <= t - delay < tiles:
                stage(t - delay)

    con_copy.wait()
    for i in range(tiles):
        out_copy(i).wait()


def on_device(
    nb, nc,
    var_feat, con_feat, slot_column_block, slot_constraint_block, block_count, incidence_coefficients,
    con_first, con_bias, con_second, con_third, con_gain, con_shift,
    var_first, var_bias, var_second, var_third, var_gain, var_shift,
):
    width = var_feat.shape[1]
    slots = slot_column_block.shape[0]
    size = incidence_coefficients.shape[1]
    cols = var_feat.shape[0] // size
    rows = con_feat.shape[0]
    rblocks = 2 * nc * (rows // size)
    early = slots // CHUNK // 2 * CHUNK
    fpairs = -(-(slots - early + rblocks) // (2 * FORWARD)) * FORWARD * 2
    pairs = -(-(slots + cols) // (2 * BACK)) * BACK
    lanes = -(-max(2 * pairs, 2 * fpairs, 2 * rblocks) // 128) * 128
    chunks = slots // CHUNK
    dims = (nb, nc, slots, size, cols, fpairs, pairs, lanes, chunks)
    vmem = pl.BlockSpec(memory_space=pltpu.VMEM)
    hbm = pl.BlockSpec(memory_space=pl.ANY)
    row = lambda v: v.reshape(1, -1)
    con_weights = (con_first, row(con_bias), con_second, con_third, row(con_gain), row(con_shift))
    var_weights = (var_first, row(var_bias), var_second, var_third, row(var_gain), row(var_shift))
    held = lambda v: pltpu.with_memory_space_constraint(v, pltpu.HBM)
    like = lambda v: pltpu.VMEM(v.shape, v.dtype)
    handed = pl.pallas_call(
        functools.partial(kernel, dims),
        out_shape=(
            pltpu.VMEM(con_feat.shape, BF16),
            pltpu.VMEM(var_feat.shape, BF16),
            like(var_feat),
            *(like(w) for w in var_weights),
        ),
        in_specs=[hbm] * 2 + [pl.BlockSpec(memory_space=pltpu.SMEM)] + [hbm] * 15,
        out_specs=(vmem,) * 9,
        scratch_shapes=[
            pltpu.VMEM((1, slots), jnp.int32),
            pltpu.VMEM((1, slots), jnp.int32),
            like(con_feat),
            *(like(w) for w in con_weights),
            pltpu.VMEM((slots, size, size), jnp.int32),
            pltpu.VMEM((slots + 1, size, size), FP8),
            pltpu.VMEM((max(fpairs, pairs), size, width), F32),
            pltpu.VMEM((pairs, size, 2 * size), FP8),
            pltpu.VMEM((cols, size, 2 * width), FP8),
            pltpu.VMEM((2 * nc, rows, width), BF16),
            pltpu.VMEM((2 * nc, rows, width), BF16),
            pltpu.VMEM((2 * nc, rows, width), BF16),
            pltpu.VMEM((rblocks, size, 2 * width), FP8),
            pltpu.VMEM((rows, width), BF16),
            pltpu.VMEM((8, lanes), jnp.int32),
            pltpu.SMEM((8, lanes), jnp.int32),
            pltpu.VMEM((8, lanes), jnp.int32),
            pltpu.SMEM((8, lanes), jnp.int32),
            pltpu.SemaphoreType.DMA((chunks,)),
            pltpu.SemaphoreType.DMA,
            pltpu.SemaphoreType.DMA((2,)),
            pltpu.SemaphoreType.DMA((13,)),
            pltpu.SemaphoreType.DMA((2,)),
            pltpu.SemaphoreType.DMA((2 * nc,)),
            pltpu.SemaphoreType.DMA((2 * nc,)),
            pltpu.SemaphoreType.DMA((2 * nc,)),
            pltpu.SemaphoreType.DMA((2 * nc,)),
        ],
        compiler_params=pltpu.CompilerParams(
            collective_id=0, has_side_effects=True, vmem_limit_bytes=48 * 1024 * 1024),
        name="layer",
    )(
        *map(held, (row(slot_column_block), row(slot_constraint_block))), block_count,
        *map(held, (var_feat, con_feat, incidence_coefficients, *con_weights, *var_weights)),
    )
    con_new, agg, feat, *weights = (pltpu.with_memory_space_constraint(v, pltpu.VMEM) for v in handed)
    return pl.pallas_call(
        column_kernel,
        out_shape=(
            jax.ShapeDtypeStruct(con_feat.shape, BF16),
            jax.ShapeDtypeStruct(var_feat.shape, BF16),
        ),
        in_specs=[vmem] * 9,
        out_specs=(hbm, hbm),
        scratch_shapes=[
            pltpu.VMEM(var_feat.shape, BF16),
            pltpu.VMEM((2, TILE, var_first.shape[1]), BF16),
            pltpu.VMEM((2, TILE, var_second.shape[1]), BF16),
            pltpu.VMEM((2, TILE, width), F32),
            pltpu.SemaphoreType.DMA((var_feat.shape[0] // TILE,)),
            pltpu.SemaphoreType.DMA,
        ],
        compiler_params=pltpu.CompilerParams(vmem_limit_bytes=32 * 1024 * 1024),
        name="columns",
    )(feat, agg, con_new, *weights)


def solution(mesh):
    both = P(("band", "cuts"))
    wide = P(("band", "cuts"), None)
    in_specs = (wide, wide, both, both, both, P(("band", "cuts"), None, None)) + (P(),) * 12
    body = functools.partial(on_device, mesh.shape["band"], mesh.shape["cuts"])
    return jax.shard_map(body, mesh=mesh, in_specs=in_specs, out_specs=(wide, wide), check_vma=False)
```

```python
import functools
import math

import jax
import jax.numpy as jnp
from jax import lax
from jax.experimental import pallas as pl
from jax.experimental.pallas import tpu as pltpu
from jax.sharding import PartitionSpec as P

EPS = 1e-05
F32 = jnp.float32
BF16 = jnp.bfloat16
MESH = pl.DeviceIdType.MESH
CHUNK = 16
UNROLL = 8
BACK = 50
PAIR = 5
BASE = 4
AHEAD = 4
TILE = 512


def layer_norm(values, gain, offset):
    center = values - jnp.mean(values, axis=-1, keepdims=True)
    spread = jnp.mean(center * center, axis=-1, keepdims=True)
    return center * lax.rsqrt(spread + EPS) * gain + offset


def node_update(feats, scaled_agg, w_first, bias, w_second, w_third, gain, offset):
    joined = jnp.concatenate([feats, scaled_agg.astype(BF16)], axis=1)
    hidden = jnp.maximum(jnp.dot(joined, w_first, preferred_element_type=F32) + bias, 0.0).astype(BF16)
    middle = jnp.maximum(jnp.dot(hidden, w_second, preferred_element_type=F32), 0.0).astype(BF16)
    output = jnp.dot(middle, w_third, preferred_element_type=F32)
    return layer_norm(feats.astype(F32) + output, gain, offset).astype(BF16)


def order_rows(key_row, key_col, other_col, live_row, live_col, lanes, keys, starts, empty):
    slots = key_col.shape[0]
    iota = lambda shape, axis: lax.broadcasted_iota(jnp.int32, shape, axis)

    def by_group(key, values):
        out = values[0]
        for g in range(1, len(values)):
            out = jnp.where(key >= g * keys, values[g], out)
        return out

    floors = tuple(g * keys for g in range(len(starts)))
    lane = iota((slots, lanes), 1)
    before = (key_row == key_col) & (iota((slots, slots), 1) < iota((slots, slots), 0))
    within = jnp.sum(jnp.where(before, live_row, 0), axis=1, keepdims=True)
    counts = jnp.sum(jnp.where(lane == key_col, live_col, 0), axis=0, keepdims=True)
    counts_col = jnp.sum(jnp.where(iota((lanes, slots), 0) == key_row, live_row, 0), axis=1, keepdims=True)
    steps, steps_col = (counts + 1) >> 1, (counts_col + 1) >> 1
    chosen = (lane < key_col) & (lane >= by_group(key_col, floors))
    base_col = jnp.sum(jnp.where(chosen, steps, 0), axis=1, keepdims=True) + by_group(key_col, starts)
    place = jnp.where(live_col > 0, base_col * 2 + within, -1)
    hit = place == lane
    index = jnp.sum(jnp.where(hit, iota((slots, lanes), 0) - slots, 0), axis=0, keepdims=True) + slots
    other = jnp.sum(jnp.where(hit, other_col, 0), axis=0, keepdims=True)
    opens = (place == lane * 2) & (within == 0)
    carry = 1 - jnp.sum(jnp.where(opens, 1, 0), axis=0, keepdims=True)
    above, below = iota((lanes, lanes), 0), iota((1, lanes), 1)
    upto = (above <= below) & (above >= by_group(below, floors))
    ends = jnp.sum(jnp.where(upto, steps_col, 0), axis=0, keepdims=True) + by_group(below, starts)
    last = jnp.where(counts > 0, ends - 1, empty)
    rows = [index, other, carry, last]
    return jnp.concatenate(rows + [jnp.zeros((1, lanes), jnp.int32)] * (8 - len(rows)), axis=0)


def kernel(
    dims,
    cb_hbm, rb_hbm, count_s, vf_hbm, cf_hbm, coef_hbm,
    cw1_hbm, cbias_hbm, cw2_hbm, cw3_hbm, cgain_hbm, cshift_hbm,
    vw1_hbm, vbias_hbm, vw2_hbm, vw3_hbm, vgain_hbm, vshift_hbm,
    con_out, sums, base, feat, order_out, vw2, vw3, vgain, vshift,
    cb_v, rb_v, cf, cw1, cbias, cw2, cw3, cgain, cshift, vw1, vbias,
    raw, half, scan, paired, part, arrive, window, mixed, conbuf, orderf_v, orderf_s, orderb_v, orderb_s,
    raw_sem, feat_sem, small_sem, weight_sem, order_sem, psend, precv, wsend, wrecv,
):
    nb, nc, slots, size, cols, lanes, groups, steps, pairs = dims
    chunks = sum(groups)
    band = lax.axis_index("band")
    cut = lax.axis_index("cuts")
    has_next = band < nb - 1
    has_prev = band > 0
    width = feat.shape[2]
    cores = 2 if nc % 2 == 0 else 1
    chips = nc // cores
    chip, core = cut // cores, lax.rem(cut, cores)

    def member(far, which):
        return lax.rem(chip + far, chips) * cores + which

    far_first = [member(f, c) for f in range(chips - 1, 0, -1) for c in reversed(range(cores))]
    everyone = far_first + [member(0, c) for c in reversed(range(cores))]
    others = far_first + [member(0, cores - 1 - core)][: cores - 1]

    small = [
        pltpu.make_async_copy(src, dst, small_sem.at[i])
        for i, (src, dst) in enumerate(((cb_hbm, cb_v), (rb_hbm, rb_v)))
    ]
    for copy in small:
        copy.start()

    def raw_copy(i):
        piece = pl.ds(i * CHUNK, CHUNK)
        return pltpu.make_async_copy(coef_hbm.at[piece], raw.at[piece], raw_sem.at[i])

    for i in range(AHEAD):
        raw_copy(i).start()
    feat_copy = pltpu.make_async_copy(vf_hbm, feat, feat_sem)
    feat_copy.start()
    weights = [
        pltpu.make_async_copy(src, dst, weight_sem.at[i])
        for i, (src, dst) in enumerate((
            (cf_hbm, cf), (cw1_hbm, cw1), (cbias_hbm, cbias), (cw2_hbm, cw2), (cw3_hbm, cw3),
            (cgain_hbm, cgain), (cshift_hbm, cshift), (vw1_hbm, vw1), (vbias_hbm, vbias), (vw2_hbm, vw2),
            (vw3_hbm, vw3), (vgain_hbm, vgain), (vshift_hbm, vshift)))
    ]
    barrier = pltpu.get_barrier_semaphore()
    for d in range(1, nc):
        pl.semaphore_signal(barrier, inc=1, device_id=(band, lax.rem(cut + d, nc)), device_id_type=MESH)

    @pl.when(has_next)
    def _():
        for d in range(nc):
            pl.semaphore_signal(barrier, inc=1, device_id=(band + 1, lax.rem(cut + d, nc)), device_id_type=MESH)

    @pl.when(has_prev)
    def _():
        for d in range(nc):
            pl.semaphore_signal(barrier, inc=1, device_id=(band - 1, lax.rem(cut + d, nc)), device_id_type=MESH)

    half[slots] = jnp.zeros((size, size), BF16)
    scan[sum(steps)] = jnp.zeros((size, width), F32)
    sums[pairs] = jnp.zeros(sums.shape[1:], F32)

    @pl.when(jnp.logical_not(has_prev))
    def _():
        arrive[pl.ds(nc, nc)] = jnp.zeros((nc,) + arrive.shape[1:], BF16)

    @pl.when(jnp.logical_not(has_next))
    def _():
        window[pl.ds(nc, nc)] = jnp.zeros((nc,) + window.shape[1:], BF16)

    for copy in small:
        copy.wait()
    row_c = cb_v[...]
    row_r = rb_v[...]
    diagonal = lax.broadcasted_iota(jnp.int32, (slots, slots), 0) == lax.broadcasted_iota(jnp.int32, (slots, slots), 1)
    col_c = jnp.sum(jnp.where(diagonal, row_c, 0), axis=1, keepdims=True)
    col_r = jnp.sum(jnp.where(diagonal, row_r, 0), axis=1, keepdims=True)
    count = count_s[0]
    slot_row = lax.broadcasted_iota(jnp.int32, (1, slots), 1)
    slot_col = lax.broadcasted_iota(jnp.int32, (slots, 1), 0)
    live_row = jnp.where(slot_row < count, 1, 0)
    live_col = jnp.where(slot_col < count, 1, 0)
    blocks = part.shape[1] // size
    keys = 2 * nc * blocks
    bounds = [CHUNK * sum(groups[:g]) for g in range(1, len(groups))]
    starts = tuple(sum(steps[:g]) for g in range(len(groups)))
    late_row = sum(jnp.where(slot_row >= b, keys, 0) for b in bounds)
    late_col = sum(jnp.where(slot_col >= b, keys, 0) for b in bounds)
    orderf_v[...] = order_rows(
        row_r + late_row, col_r + late_col, col_c, live_row, live_col, lanes, keys, starts, sum(steps))
    orderf_copy = pltpu.make_async_copy(orderf_v, orderf_s, order_sem.at[0])
    orderf_copy.start()

    def convert(i):
        raw_copy(i).wait()

        @pl.when(i + AHEAD < chunks)
        def _():
            raw_copy(i + AHEAD).start()

        for u in range(CHUNK):
            half[i * CHUNK + u] = raw[i * CHUNK + u].astype(F32).astype(BF16)

    def convert_step(i, _):
        convert(i)
        return 0

    lax.fori_loop(0, groups[0], convert_step, 0)
    feat_copy.wait()
    orderf_copy.wait()

    carry = jnp.zeros((size, width), F32)
    for g, start in enumerate(starts):
        turns = groups[g + 1] if g + 1 < len(groups) else 1
        chunk = sum(groups[: g + 1])
        unroll = steps[g] // turns

        def forward(k, carry, start=start, unroll=unroll, chunk=chunk, more=g + 1 < len(groups)):
            for u in range(unroll):
                at = start + k * unroll + u
                left = jnp.concatenate([half[orderf_s[0, 2 * at]], half[orderf_s[0, 2 * at + 1]]], axis=1)
                right = jnp.concatenate(
                    [feat[orderf_s[1, 2 * at]], feat[orderf_s[1, 2 * at + 1]]], axis=0)
                term = jnp.dot(left, right, preferred_element_type=F32)
                carry = carry * orderf_s[2, at].astype(F32) + term
                scan[at] = carry
            if more:
                convert(chunk + k)
            return carry

        carry = lax.fori_loop(0, turns, forward, carry)
        if g == 0:
            for copy in weights:
                copy.start()

    def fill(q):
        for e in range(blocks):
            r = q * blocks + e
            total = scan[orderf_s[3, r]]
            for g in range(1, len(groups)):
                total += scan[orderf_s[3, g * keys + r]]
            part[q, e * size : (e + 1) * size] = total.astype(BF16)

    def part_send(i, to, ahead):
        return pltpu.make_async_remote_copy(
            src_ref=part.at[ahead * nc + to], dst_ref=arrive.at[ahead * nc + cut],
            send_sem=psend.at[ahead * nc + i], recv_sem=precv.at[ahead * nc + cut],
            device_id=(band + ahead, to), device_id_type=MESH)

    def part_wait(src, ahead):
        pltpu.make_async_remote_copy(
            src_ref=part.at[0], dst_ref=arrive.at[ahead * nc + src],
            send_sem=psend.at[0], recv_sem=precv.at[ahead * nc + src],
            device_id=(band, cut), device_id_type=MESH).wait_recv()

    for q in range(2 * nc):
        fill(q)

    expected = (nc - 1) + jnp.where(has_next, nc, 0) + jnp.where(has_prev, nc, 0)
    pl.semaphore_wait(barrier, expected)

    @pl.when(has_next)
    def _():
        for i, to in enumerate(everyone):
            part_send(i, to, 1).start()

    for i, to in enumerate(others):
        part_send(i, to, 0).start()

    orderb_v[...] = order_rows(row_c, col_c, col_r, live_row, live_col, lanes, lanes, (0,), pairs)
    orderb_copy = pltpu.make_async_copy(orderb_v, orderb_s, order_sem.at[1])
    orderb_copy.start()
    order_copy = pltpu.make_async_copy(orderb_v, order_out, order_sem.at[2])
    order_copy.start()
    for copy in weights:
        copy.wait()
    orderb_copy.wait()
    order_copy.wait()

    def pair_up(p, _):
        for u in range(PAIR):
            k = p * PAIR + u
            paired[k, :, :size] = half[orderb_s[0, 2 * k]].T
            paired[k, :, size:] = half[orderb_s[0, 2 * k + 1]].T
        return 0

    lax.fori_loop(0, pairs // PAIR, pair_up, 0)

    total = part[cut].astype(F32)
    for d in range(1, nc):
        src = lax.rem(cut + d, nc)
        part_wait(src, 0)
        total += arrive[src].astype(F32)

    @pl.when(has_prev)
    def _():
        for src in range(nc):
            part_wait(src, 1)

    for src in range(nc):
        total += arrive[nc + src].astype(F32)

    con_new = node_update(
        cf[...], total * (1.0 / math.sqrt(size * slots)), cw1[...], cbias[...], cw2[...], cw3[...], cgain[...], cshift[...])
    conbuf[...] = con_new
    window[cut] = con_new

    def win_send(i, to, back):
        return pltpu.make_async_remote_copy(
            src_ref=conbuf, dst_ref=window.at[back * nc + cut],
            send_sem=wsend.at[back * nc + i], recv_sem=wrecv.at[back * nc + cut],
            device_id=(band - back, to), device_id_type=MESH)

    def win_wait(src, back):
        pltpu.make_async_remote_copy(
            src_ref=conbuf, dst_ref=window.at[back * nc + src],
            send_sem=wsend.at[0], recv_sem=wrecv.at[back * nc + src],
            device_id=(band, cut), device_id_type=MESH).wait_recv()

    @pl.when(has_prev)
    def _():
        for i, to in enumerate(everyone):
            win_send(i, to, 1).start()

    for i, to in enumerate(others):
        win_send(i, to, 0).start()

    con_out[...] = con_new

    def base_step(i, _):
        for u in range(BASE):
            c = i * BASE + u
            base[c] = jnp.dot(feat[c], vw1[:width], preferred_element_type=F32) + vbias[...]
        return 0

    lax.fori_loop(0, cols // BASE, base_step, 0)

    def mix(q):
        for e in range(blocks):
            product = jnp.dot(window[q, e * size : (e + 1) * size], vw1[width:], preferred_element_type=F32)
            mixed[q * blocks + e] = (product * (1.0 / math.sqrt(4 * size))).astype(BF16)

    for d in range(1, nc):
        win_wait(lax.rem(cut + d, nc), 0)
    for q in range(nc):
        mix(q)

    @pl.when(has_next)
    def _():
        for src in range(nc):
            win_wait(src, 1)

    for q in range(nc, 2 * nc):
        mix(q)

    def back(k, carry):
        for u in range(BACK):
            at = k * BACK + u
            right = jnp.concatenate([mixed[orderb_s[1, 2 * at]], mixed[orderb_s[1, 2 * at + 1]]], axis=0)
            term = jnp.dot(paired[at], right, preferred_element_type=F32)
            carry = carry * orderb_s[2, at].astype(F32) + term
            sums[at] = carry
        return carry

    lax.fori_loop(0, pairs // BACK, back, jnp.zeros(sums.shape[1:], F32))

    @pl.when(has_next)
    def _():
        for i, to in enumerate(everyone):
            part_send(i, to, 1).wait_send()

    @pl.when(has_prev)
    def _():
        for i, to in enumerate(everyone):
            win_send(i, to, 1).wait_send()

    for i, to in enumerate(others):
        part_send(i, to, 0).wait_send()
        win_send(i, to, 0).wait_send()


def column_kernel(
    size, con, sums, base, feat, order_s, vw2, vw3, vgain, vshift, con_out, var_out,
    result, hidden, middle, output, out_sem, con_sem,
):
    con_copy = pltpu.make_async_copy(con, con_out, con_sem)
    con_copy.start()
    per = TILE // size
    tiles = feat.shape[0] // per
    piece = lambda i: pl.ds(i * TILE, TILE)

    def out_copy(i):
        return pltpu.make_async_copy(result.at[piece(i)], var_out.at[piece(i)], out_sem.at[i])

    def first(i):
        for e in range(per):
            c = i * per + e
            total = sums[order_s[3, c]] + base[c]
            hidden[i % 2, e * size : (e + 1) * size] = jnp.maximum(total, 0.0).astype(BF16)

    def second(i):
        sums = jnp.dot(hidden[i % 2], vw2[...], preferred_element_type=F32)
        middle[i % 2] = jnp.maximum(sums, 0.0).astype(BF16)

    def third(i):
        sums = jnp.dot(middle[i % 2], vw3[...], preferred_element_type=F32)
        output[i % 2] = feat[i * per : (i + 1) * per].reshape(sums.shape).astype(F32) + sums

    def norm(i):
        result[piece(i)] = layer_norm(output[i % 2], vgain[...], vshift[...]).astype(BF16)
        out_copy(i).start()

    stages = (norm, 3), (third, 2), (second, 1), (first, 0)
    for t in range(tiles + len(stages) - 1):
        for stage, delay in stages:
            if 0 <= t - delay < tiles:
                stage(t - delay)

    con_copy.wait()
    for i in range(tiles):
        out_copy(i).wait()


def on_device(
    nb, nc,
    var_feat, con_feat, slot_column_block, slot_constraint_block, block_count, incidence_coefficients,
    con_first, con_bias, con_second, con_third, con_gain, con_shift,
    var_first, var_bias, var_second, var_third, var_gain, var_shift,
):
    width = var_feat.shape[1]
    slots = slot_column_block.shape[0]
    size = incidence_coefficients.shape[1]
    cols = var_feat.shape[0] // size
    rows = con_feat.shape[0]
    rblocks = 2 * nc * (rows // size)
    chunks = slots // CHUNK
    tail = chunks // 5
    groups = (chunks - 2 * (chunks - tail) // 4 - tail, 2 * (chunks - tail) // 4, tail)
    turns = groups[1:] + (1,)
    steps = tuple(-(-(g * CHUNK + rblocks) // (2 * t)) * t for g, t in zip(groups, turns))
    pairs = -(-(slots + cols) // (2 * BACK)) * BACK
    lanes = -(-max(2 * pairs, 2 * sum(steps), 3 * rblocks) // 128) * 128
    dims = (nb, nc, slots, size, cols, lanes, groups, steps, pairs)
    vmem = pl.BlockSpec(memory_space=pltpu.VMEM)
    smem = pl.BlockSpec(memory_space=pltpu.SMEM)
    hbm = pl.BlockSpec(memory_space=pl.ANY)
    row = lambda v: v.reshape(1, -1)
    con_weights = (con_first, row(con_bias), con_second, con_third, row(con_gain), row(con_shift))
    var_weights = (var_first, row(var_bias), var_second, var_third, row(var_gain), row(var_shift))
    held = lambda v: pltpu.with_memory_space_constraint(v, pltpu.HBM)
    like = lambda v: pltpu.VMEM(v.shape, v.dtype)
    hid = var_first.shape[1]
    handed = pl.pallas_call(
        functools.partial(kernel, dims),
        out_shape=(
            like(con_feat),
            pltpu.VMEM((pairs + 1, size, hid), F32),
            pltpu.VMEM((cols, size, hid), F32),
            pltpu.VMEM((cols, size, width), BF16),
            pltpu.SMEM((8, lanes), jnp.int32),
            *(like(w) for w in var_weights[2:]),
        ),
        in_specs=[hbm] * 2 + [smem] + [hbm] * 15,
        out_specs=(vmem,) * 4 + (smem,) + (vmem,) * 4,
        scratch_shapes=[
            pltpu.VMEM((1, slots), jnp.int32),
            pltpu.VMEM((1, slots), jnp.int32),
            like(con_feat),
            *(like(w) for w in con_weights + var_weights[:2]),
            pltpu.VMEM((slots, size, size), jnp.int32),
            pltpu.VMEM((slots + 1, size, size), BF16),
            pltpu.VMEM((sum(steps) + 1, size, width), F32),
            pltpu.VMEM((pairs, size, 2 * size), BF16),
            pltpu.VMEM((2 * nc, rows, width), BF16),
            pltpu.VMEM((2 * nc, rows, width), BF16),
            pltpu.VMEM((2 * nc, rows, width), BF16),
            pltpu.VMEM((rblocks, size, hid), BF16),
            pltpu.VMEM((rows, width), BF16),
            pltpu.VMEM((8, lanes), jnp.int32),
            pltpu.SMEM((8, lanes), jnp.int32),
            pltpu.VMEM((8, lanes), jnp.int32),
            pltpu.SMEM((8, lanes), jnp.int32),
            pltpu.SemaphoreType.DMA((chunks,)),
            pltpu.SemaphoreType.DMA,
            pltpu.SemaphoreType.DMA((2,)),
            pltpu.SemaphoreType.DMA((13,)),
            pltpu.SemaphoreType.DMA((3,)),
            pltpu.SemaphoreType.DMA((2 * nc,)),
            pltpu.SemaphoreType.DMA((2 * nc,)),
            pltpu.SemaphoreType.DMA((2 * nc,)),
            pltpu.SemaphoreType.DMA((2 * nc,)),
        ],
        compiler_params=pltpu.CompilerParams(
            collective_id=0, has_side_effects=True, vmem_limit_bytes=37 * 1024 * 1024),
        name="layer",
    )(
        *map(held, (row(slot_column_block), row(slot_constraint_block))), block_count,
        *map(held, (var_feat.reshape(cols, size, width), con_feat, incidence_coefficients, *con_weights, *var_weights)),
    )
    spaces = (pltpu.VMEM,) * 4 + (pltpu.SMEM,) + (pltpu.VMEM,) * 4
    return pl.pallas_call(
        functools.partial(column_kernel, size),
        out_shape=(
            jax.ShapeDtypeStruct(con_feat.shape, BF16),
            jax.ShapeDtypeStruct(var_feat.shape, BF16),
        ),
        in_specs=[vmem] * 4 + [smem] + [vmem] * 4,
        out_specs=(hbm, hbm),
        scratch_shapes=[
            pltpu.VMEM(var_feat.shape, BF16),
            pltpu.VMEM((2, TILE, hid), BF16),
            pltpu.VMEM((2, TILE, var_second.shape[1]), BF16),
            pltpu.VMEM((2, TILE, width), F32),
            pltpu.SemaphoreType.DMA((var_feat.shape[0] // TILE,)),
            pltpu.SemaphoreType.DMA,
        ],
        compiler_params=pltpu.CompilerParams(vmem_limit_bytes=8 * 1024 * 1024),
        name="columns",
    )(*map(pltpu.with_memory_space_constraint, handed, spaces))


def solution(mesh):
    both = P(("band", "cuts"))
    wide = P(("band", "cuts"), None)
    in_specs = (wide, wide, both, both, both, P(("band", "cuts"), None, None)) + (P(),) * 12
    body = functools.partial(on_device, mesh.shape["band"], mesh.shape["cuts"])
    return jax.shard_map(body, mesh=mesh, in_specs=in_specs, out_specs=(wide, wide), check_vma=False)
```

```python
import functools
import math

import jax
import jax.numpy as jnp
from jax import lax
from jax.experimental import pallas as pl
from jax.experimental.pallas import tpu as pltpu
from jax.sharding import PartitionSpec as P

EPS = 1e-05
F32 = jnp.float32
BF16 = jnp.bfloat16
MESH = pl.DeviceIdType.MESH
CHUNK = 16
UNROLL = 8
BACK = 100
PAIR = 5
BASE = 4
AHEAD = 4
TILE = 512


def relu(values):
    return jnp.maximum(values.astype(BF16), jnp.zeros((), BF16))


def layer_norm(values, gain, offset):
    center = values - jnp.mean(values, axis=-1, keepdims=True)
    spread = jnp.mean(center * center, axis=-1, keepdims=True)
    return center * lax.rsqrt(spread + EPS) * gain + offset


def node_update(feats, scaled_agg, w_first, bias, w_second, w_third, gain, offset):
    joined = jnp.concatenate([feats, scaled_agg.astype(BF16)], axis=1)
    hidden = relu(jnp.dot(joined, w_first, preferred_element_type=F32) + bias)
    middle = relu(jnp.dot(hidden, w_second, preferred_element_type=F32))
    output = jnp.dot(middle, w_third, preferred_element_type=F32)
    return layer_norm(feats.astype(F32) + output, gain, offset).astype(BF16)


def order_rows(key_row, key_col, other_col, live_row, live_col, lanes, keys, starts, empty):
    slots = key_col.shape[0]
    iota = lambda shape, axis: lax.broadcasted_iota(jnp.int32, shape, axis)

    def by_group(key, values):
        out = values[0]
        for g in range(1, len(values)):
            out = jnp.where(key >= g * keys, values[g], out)
        return out

    floors = tuple(g * keys for g in range(len(starts)))
    lane = iota((slots, lanes), 1)
    before = (key_row == key_col) & (iota((slots, slots), 1) < iota((slots, slots), 0))
    within = jnp.sum(jnp.where(before, live_row, 0), axis=1, keepdims=True)
    counts = jnp.sum(jnp.where(lane == key_col, live_col, 0), axis=0, keepdims=True)
    counts_col = jnp.sum(jnp.where(iota((lanes, slots), 0) == key_row, live_row, 0), axis=1, keepdims=True)
    steps, steps_col = (counts + 1) >> 1, (counts_col + 1) >> 1
    chosen = (lane < key_col) & (lane >= by_group(key_col, floors))
    base_col = jnp.sum(jnp.where(chosen, steps, 0), axis=1, keepdims=True) + by_group(key_col, starts)
    place = jnp.where(live_col > 0, base_col * 2 + within, -1)
    hit = place == lane
    index = jnp.sum(jnp.where(hit, iota((slots, lanes), 0) - slots, 0), axis=0, keepdims=True) + slots
    other = jnp.sum(jnp.where(hit, other_col, 0), axis=0, keepdims=True)
    opens = (place == lane * 2) & (within == 0)
    carry = 1 - jnp.sum(jnp.where(opens, 1, 0), axis=0, keepdims=True)
    above, below = iota((lanes, lanes), 0), iota((1, lanes), 1)
    upto = (above <= below) & (above >= by_group(below, floors))
    ends = jnp.sum(jnp.where(upto, steps_col, 0), axis=0, keepdims=True) + by_group(below, starts)
    last = jnp.where(counts > 0, ends - 1, empty)
    rows = [index, other, carry, last]
    return jnp.concatenate(rows + [jnp.zeros((1, lanes), jnp.int32)] * (8 - len(rows)), axis=0)


def kernel(
    dims,
    cb_hbm, rb_hbm, count_s, vf_hbm, cf_hbm, coef_hbm,
    cw1_hbm, cbias_hbm, cw2_hbm, cw3_hbm, cgain_hbm, cshift_hbm,
    vw1_hbm, vbias_hbm, vw2_hbm, vw3_hbm, vgain_hbm, vshift_hbm,
    con_out, sums, base, feat, order_out, vw2, vw3, vgain, vshift,
    cb_v, rb_v, cf, cw1, cbias, cw2, cw3, cgain, cshift, vw1, vbias,
    raw, half, scan, paired, part, arrive, window, mixed, conbuf, orderf_v, orderf_s, orderb_v, orderb_s,
    raw_sem, feat_sem, small_sem, weight_sem, order_sem, psend, precv, wsend, wrecv,
):
    nb, nc, slots, size, cols, lanes, groups, steps, pairs = dims
    chunks = sum(groups)
    band = lax.axis_index("band")
    cut = lax.axis_index("cuts")
    has_next = band < nb - 1
    has_prev = band > 0
    width = feat.shape[2]
    cores = 2 if nc % 2 == 0 else 1
    chips = nc // cores
    chip, core = cut // cores, lax.rem(cut, cores)

    def member(far, which):
        return lax.rem(chip + far, chips) * cores + which

    far_first = [member(f, c) for f in range(chips - 1, 0, -1) for c in reversed(range(cores))]
    everyone = far_first + [member(0, c) for c in reversed(range(cores))]
    others = far_first + [member(0, cores - 1 - core)][: cores - 1]

    small = [
        pltpu.make_async_copy(src, dst, small_sem.at[i])
        for i, (src, dst) in enumerate(((cb_hbm, cb_v), (rb_hbm, rb_v)))
    ]
    for copy in small:
        copy.start()

    def raw_copy(i):
        piece = pl.ds(i * CHUNK, CHUNK)
        return pltpu.make_async_copy(coef_hbm.at[piece], raw.at[piece], raw_sem.at[i])

    for i in range(AHEAD):
        raw_copy(i).start()
    feat_copy = pltpu.make_async_copy(vf_hbm, feat, feat_sem)
    feat_copy.start()
    weights = [
        pltpu.make_async_copy(src, dst, weight_sem.at[i])
        for i, (src, dst) in enumerate((
            (cf_hbm, cf), (cw1_hbm, cw1), (cbias_hbm, cbias), (cw2_hbm, cw2), (cw3_hbm, cw3),
            (cgain_hbm, cgain), (cshift_hbm, cshift), (vw1_hbm, vw1), (vbias_hbm, vbias), (vw2_hbm, vw2),
            (vw3_hbm, vw3), (vgain_hbm, vgain), (vshift_hbm, vshift)))
    ]
    barrier = pltpu.get_barrier_semaphore()
    for d in range(1, nc):
        pl.semaphore_signal(barrier, inc=1, device_id=(band, lax.rem(cut + d, nc)), device_id_type=MESH)

    @pl.when(has_next)
    def _():
        for d in range(nc):
            pl.semaphore_signal(barrier, inc=1, device_id=(band + 1, lax.rem(cut + d, nc)), device_id_type=MESH)

    @pl.when(has_prev)
    def _():
        for d in range(nc):
            pl.semaphore_signal(barrier, inc=1, device_id=(band - 1, lax.rem(cut + d, nc)), device_id_type=MESH)

    half[slots] = jnp.zeros((size, size), BF16)
    scan[sum(steps)] = jnp.zeros((size, width), F32)
    sums[pairs] = jnp.zeros(sums.shape[1:], F32)

    @pl.when(jnp.logical_not(has_prev))
    def _():
        arrive[pl.ds(nc, nc)] = jnp.zeros((nc,) + arrive.shape[1:], BF16)

    @pl.when(jnp.logical_not(has_next))
    def _():
        window[pl.ds(nc, nc)] = jnp.zeros((nc,) + window.shape[1:], BF16)

    for copy in small:
        copy.wait()
    row_c = cb_v[...]
    row_r = rb_v[...]
    diagonal = lax.broadcasted_iota(jnp.int32, (slots, slots), 0) == lax.broadcasted_iota(jnp.int32, (slots, slots), 1)
    col_c = jnp.sum(jnp.where(diagonal, row_c, 0), axis=1, keepdims=True)
    col_r = jnp.sum(jnp.where(diagonal, row_r, 0), axis=1, keepdims=True)
    count = count_s[0]
    slot_row = lax.broadcasted_iota(jnp.int32, (1, slots), 1)
    slot_col = lax.broadcasted_iota(jnp.int32, (slots, 1), 0)
    live_row = jnp.where(slot_row < count, 1, 0)
    live_col = jnp.where(slot_col < count, 1, 0)
    blocks = part.shape[1] // size
    keys = 2 * nc * blocks
    bounds = [CHUNK * sum(groups[:g]) for g in range(1, len(groups))]
    starts = tuple(sum(steps[:g]) for g in range(len(groups)))
    late_row = sum(jnp.where(slot_row >= b, keys, 0) for b in bounds)
    late_col = sum(jnp.where(slot_col >= b, keys, 0) for b in bounds)
    orderf_v[...] = order_rows(
        row_r + late_row, col_r + late_col, col_c, live_row, live_col, lanes, keys, starts, sum(steps))
    orderf_copy = pltpu.make_async_copy(orderf_v, orderf_s, order_sem.at[0])
    orderf_copy.start()

    def convert(i):
        raw_copy(i).wait()

        @pl.when(i + AHEAD < chunks)
        def _():
            raw_copy(i + AHEAD).start()

        for u in range(CHUNK):
            half[i * CHUNK + u] = raw[i * CHUNK + u].astype(F32).astype(BF16)

    def convert_step(i, _):
        convert(i)
        return 0

    lax.fori_loop(0, groups[0], convert_step, 0)
    feat_copy.wait()
    orderf_copy.wait()

    carry = jnp.zeros((size, width), F32)
    for g, start in enumerate(starts):
        turns = groups[g + 1] if g + 1 < len(groups) else 1
        chunk = sum(groups[: g + 1])
        unroll = steps[g] // turns

        def forward(k, carry, start=start, unroll=unroll, chunk=chunk, more=g + 1 < len(groups)):
            for u in range(unroll):
                at = start + k * unroll + u
                left = jnp.concatenate([half[orderf_s[0, 2 * at]], half[orderf_s[0, 2 * at + 1]]], axis=1)
                right = jnp.concatenate(
                    [feat[orderf_s[1, 2 * at]], feat[orderf_s[1, 2 * at + 1]]], axis=0)
                term = jnp.dot(left, right, preferred_element_type=F32)
                carry = carry * orderf_s[2, at].astype(F32) + term
                scan[at] = carry
            if more:
                convert(chunk + k)
            return carry

        carry = lax.fori_loop(0, turns, forward, carry)
        if g == len(groups) - 2:
            for copy in weights:
                copy.start()

    def fill(q):
        for e in range(blocks):
            r = q * blocks + e
            total = scan[orderf_s[3, r]]
            for g in range(1, len(groups)):
                total += scan[orderf_s[3, g * keys + r]]
            part[q, e * size : (e + 1) * size] = total.astype(BF16)

    def part_send(i, to, ahead):
        return pltpu.make_async_remote_copy(
            src_ref=part.at[ahead * nc + to], dst_ref=arrive.at[ahead * nc + cut],
            send_sem=psend.at[ahead * nc + i], recv_sem=precv.at[ahead * nc + cut],
            device_id=(band + ahead, to), device_id_type=MESH)

    def part_wait(src, ahead):
        pltpu.make_async_remote_copy(
            src_ref=part.at[0], dst_ref=arrive.at[ahead * nc + src],
            send_sem=psend.at[0], recv_sem=precv.at[ahead * nc + src],
            device_id=(band, cut), device_id_type=MESH).wait_recv()

    for q in range(2 * nc):
        fill(q)

    expected = (nc - 1) + jnp.where(has_next, nc, 0) + jnp.where(has_prev, nc, 0)
    pl.semaphore_wait(barrier, expected)

    @pl.when(has_next)
    def _():
        for i, to in enumerate(everyone):
            part_send(i, to, 1).start()

    for i, to in enumerate(others):
        part_send(i, to, 0).start()

    orderb_v[...] = order_rows(row_c, col_c, col_r, live_row, live_col, lanes, lanes, (0,), pairs)
    orderb_copy = pltpu.make_async_copy(orderb_v, orderb_s, order_sem.at[1])
    orderb_copy.start()
    order_copy = pltpu.make_async_copy(orderb_v, order_out, order_sem.at[2])
    order_copy.start()
    for copy in weights:
        copy.wait()
    orderb_copy.wait()
    order_copy.wait()

    def pair_up(p, _):
        for u in range(PAIR):
            k = p * PAIR + u
            paired[k, :, :size] = half[orderb_s[0, 2 * k]].T
            paired[k, :, size:] = half[orderb_s[0, 2 * k + 1]].T
        return 0

    lax.fori_loop(0, pairs // PAIR, pair_up, 0)

    total = part[cut].astype(F32)
    for d in range(1, nc):
        src = lax.rem(cut + d, nc)
        part_wait(src, 0)
        total += arrive[src].astype(F32)

    @pl.when(has_prev)
    def _():
        for src in range(nc):
            part_wait(src, 1)

    for src in range(nc):
        total += arrive[nc + src].astype(F32)

    con_new = node_update(
        cf[...], total * (1.0 / math.sqrt(size * slots)), cw1[...], cbias[...], cw2[...], cw3[...], cgain[...], cshift[...])
    conbuf[...] = con_new
    window[cut] = con_new

    def win_send(i, to, back):
        return pltpu.make_async_remote_copy(
            src_ref=conbuf, dst_ref=window.at[back * nc + cut],
            send_sem=wsend.at[back * nc + i], recv_sem=wrecv.at[back * nc + cut],
            device_id=(band - back, to), device_id_type=MESH)

    def win_wait(src, back):
        pltpu.make_async_remote_copy(
            src_ref=conbuf, dst_ref=window.at[back * nc + src],
            send_sem=wsend.at[0], recv_sem=wrecv.at[back * nc + src],
            device_id=(band, cut), device_id_type=MESH).wait_recv()

    for i, to in enumerate(others):
        win_send(i, to, 0).start()

    @pl.when(has_prev)
    def _():
        for i, to in enumerate(everyone):
            win_send(i, to, 1).start()

    con_out[...] = con_new

    def base_step(i, _):
        for u in range(BASE):
            c = i * BASE + u
            base[c] = jnp.dot(feat[c], vw1[:width], preferred_element_type=F32) + vbias[...]
        return 0

    lax.fori_loop(0, cols // BASE, base_step, 0)

    def mix(q):
        for e in range(blocks):
            product = jnp.dot(window[q, e * size : (e + 1) * size], vw1[width:], preferred_element_type=F32)
            mixed[q * blocks + e] = (product * (1.0 / math.sqrt(4 * size))).astype(BF16)

    for d in range(1, nc):
        win_wait(lax.rem(cut + d, nc), 0)
    for q in range(nc):
        mix(q)

    @pl.when(has_next)
    def _():
        for src in range(nc):
            win_wait(src, 1)

    for q in range(nc, 2 * nc):
        mix(q)

    def back(k, carry):
        for u in range(BACK):
            at = k * BACK + u
            right = jnp.concatenate([mixed[orderb_s[1, 2 * at]], mixed[orderb_s[1, 2 * at + 1]]], axis=0)
            term = jnp.dot(paired[at], right, preferred_element_type=F32)
            carry = carry * orderb_s[2, at].astype(F32) + term
            sums[at] = carry
        return carry

    lax.fori_loop(0, pairs // BACK, back, jnp.zeros(sums.shape[1:], F32))

    @pl.when(has_next)
    def _():
        for i, to in enumerate(everyone):
            part_send(i, to, 1).wait_send()

    @pl.when(has_prev)
    def _():
        for i, to in enumerate(everyone):
            win_send(i, to, 1).wait_send()

    for i, to in enumerate(others):
        part_send(i, to, 0).wait_send()
        win_send(i, to, 0).wait_send()


def column_kernel(
    size, con, sums, base, feat, order_s, vw2, vw3, vgain, vshift, con_out, var_out,
    result, hidden, middle, output, out_sem, con_sem,
):
    con_copy = pltpu.make_async_copy(con, con_out, con_sem)
    con_copy.start()
    per = TILE // size
    tiles = feat.shape[0] // per
    piece = lambda i: pl.ds(i * TILE, TILE)

    def out_copy(i):
        return pltpu.make_async_copy(result.at[piece(i)], var_out.at[piece(i)], out_sem.at[i])

    def first(i):
        for e in range(per):
            c = i * per + e
            total = sums[order_s[3, c]] + base[c]
            hidden[i % 2, e * size : (e + 1) * size] = relu(total)

    def second(i):
        sums = jnp.dot(hidden[i % 2], vw2[...], preferred_element_type=F32)
        middle[i % 2] = relu(sums)

    def third(i):
        sums = jnp.dot(middle[i % 2], vw3[...], preferred_element_type=F32)
        output[i % 2] = feat[i * per : (i + 1) * per].reshape(sums.shape).astype(F32) + sums

    def norm(i):
        result[piece(i)] = layer_norm(output[i % 2], vgain[...], vshift[...]).astype(BF16)
        out_copy(i).start()

    stages = (norm, 3), (third, 2), (second, 1), (first, 0)
    for t in range(tiles + len(stages) - 1):
        for stage, delay in stages:
            if 0 <= t - delay < tiles:
                stage(t - delay)

    con_copy.wait()
    for i in range(tiles):
        out_copy(i).wait()


def on_device(
    nb, nc,
    var_feat, con_feat, slot_column_block, slot_constraint_block, block_count, incidence_coefficients,
    con_first, con_bias, con_second, con_third, con_gain, con_shift,
    var_first, var_bias, var_second, var_third, var_gain, var_shift,
):
    width = var_feat.shape[1]
    slots = slot_column_block.shape[0]
    size = incidence_coefficients.shape[1]
    cols = var_feat.shape[0] // size
    rows = con_feat.shape[0]
    rblocks = 2 * nc * (rows // size)
    chunks = slots // CHUNK
    tail = chunks // 5
    groups = (chunks - 2 * (chunks - tail) // 4 - tail, 2 * (chunks - tail) // 4, tail)
    turns = groups[1:] + (1,)
    steps = tuple(-(-(g * CHUNK + rblocks) // (2 * t)) * t for g, t in zip(groups, turns))
    pairs = -(-(slots + cols) // (2 * BACK)) * BACK
    lanes = -(-max(2 * pairs, 2 * sum(steps), 3 * rblocks) // 128) * 128
    dims = (nb, nc, slots, size, cols, lanes, groups, steps, pairs)
    vmem = pl.BlockSpec(memory_space=pltpu.VMEM)
    smem = pl.BlockSpec(memory_space=pltpu.SMEM)
    hbm = pl.BlockSpec(memory_space=pl.ANY)
    row = lambda v: v.reshape(1, -1)
    con_weights = (con_first, row(con_bias), con_second, con_third, row(con_gain), row(con_shift))
    var_weights = (var_first, row(var_bias), var_second, var_third, row(var_gain), row(var_shift))
    held = lambda v: pltpu.with_memory_space_constraint(v, pltpu.HBM)
    like = lambda v: pltpu.VMEM(v.shape, v.dtype)
    hid = var_first.shape[1]
    handed = pl.pallas_call(
        functools.partial(kernel, dims),
        out_shape=(
            like(con_feat),
            pltpu.VMEM((pairs + 1, size, hid), F32),
            pltpu.VMEM((cols, size, hid), F32),
            pltpu.VMEM((cols, size, width), BF16),
            pltpu.SMEM((8, lanes), jnp.int32),
            *(like(w) for w in var_weights[2:]),
        ),
        in_specs=[hbm] * 2 + [smem] + [hbm] * 15,
        out_specs=(vmem,) * 4 + (smem,) + (vmem,) * 4,
        scratch_shapes=[
            pltpu.VMEM((1, slots), jnp.int32),
            pltpu.VMEM((1, slots), jnp.int32),
            like(con_feat),
            *(like(w) for w in con_weights + var_weights[:2]),
            pltpu.VMEM((slots, size, size), jnp.int32),
            pltpu.VMEM((slots + 1, size, size), BF16),
            pltpu.VMEM((sum(steps) + 1, size, width), F32),
            pltpu.VMEM((pairs, size, 2 * size), BF16),
            pltpu.VMEM((2 * nc, rows, width), BF16),
            pltpu.VMEM((2 * nc, rows, width), BF16),
            pltpu.VMEM((2 * nc, rows, width), BF16),
            pltpu.VMEM((rblocks, size, hid), BF16),
            pltpu.VMEM((rows, width), BF16),
            pltpu.VMEM((8, lanes), jnp.int32),
            pltpu.SMEM((8, lanes), jnp.int32),
            pltpu.VMEM((8, lanes), jnp.int32),
            pltpu.SMEM((8, lanes), jnp.int32),
            pltpu.SemaphoreType.DMA((chunks,)),
            pltpu.SemaphoreType.DMA,
            pltpu.SemaphoreType.DMA((2,)),
            pltpu.SemaphoreType.DMA((13,)),
            pltpu.SemaphoreType.DMA((3,)),
            pltpu.SemaphoreType.DMA((2 * nc,)),
            pltpu.SemaphoreType.DMA((2 * nc,)),
            pltpu.SemaphoreType.DMA((2 * nc,)),
            pltpu.SemaphoreType.DMA((2 * nc,)),
        ],
        compiler_params=pltpu.CompilerParams(
            collective_id=0, has_side_effects=True, vmem_limit_bytes=37 * 1024 * 1024),
        name="layer",
    )(
        *map(held, (row(slot_column_block), row(slot_constraint_block))), block_count,
        *map(held, (var_feat.reshape(cols, size, width), con_feat, incidence_coefficients, *con_weights, *var_weights)),
    )
    spaces = (pltpu.VMEM,) * 4 + (pltpu.SMEM,) + (pltpu.VMEM,) * 4
    return pl.pallas_call(
        functools.partial(column_kernel, size),
        out_shape=(
            jax.ShapeDtypeStruct(con_feat.shape, BF16),
            jax.ShapeDtypeStruct(var_feat.shape, BF16),
        ),
        in_specs=[vmem] * 4 + [smem] + [vmem] * 4,
        out_specs=(hbm, hbm),
        scratch_shapes=[
            pltpu.VMEM(var_feat.shape, BF16),
            pltpu.VMEM((2, TILE, hid), BF16),
            pltpu.VMEM((2, TILE, var_second.shape[1]), BF16),
            pltpu.VMEM((2, TILE, width), F32),
            pltpu.SemaphoreType.DMA((var_feat.shape[0] // TILE,)),
            pltpu.SemaphoreType.DMA,
        ],
        compiler_params=pltpu.CompilerParams(vmem_limit_bytes=8 * 1024 * 1024),
        name="columns",
    )(*map(pltpu.with_memory_space_constraint, handed, spaces))


def solution(mesh):
    both = P(("band", "cuts"))
    wide = P(("band", "cuts"), None)
    in_specs = (wide, wide, both, both, both, P(("band", "cuts"), None, None)) + (P(),) * 12
    body = functools.partial(on_device, mesh.shape["band"], mesh.shape["cuts"])
    return jax.shard_map(body, mesh=mesh, in_specs=in_specs, out_specs=(wide, wide), check_vma=False)
```

```python
import functools
import math

import jax
import jax.numpy as jnp
from jax import lax
from jax.experimental import pallas as pl
from jax.experimental.pallas import tpu as pltpu
from jax.sharding import PartitionSpec as P

EPS = 1e-05
F32 = jnp.float32
BF16 = jnp.bfloat16
MESH = pl.DeviceIdType.MESH
CHUNK = 16
UNROLL = 8
BACK = 100
PAIR = 5
BASE = 4
AHEAD = 4
TILE = 512


def relu(values):
    return jnp.maximum(values.astype(BF16), jnp.zeros((), BF16))


def layer_norm(values, gain, offset):
    center = values - jnp.mean(values, axis=-1, keepdims=True)
    spread = jnp.mean(center * center, axis=-1, keepdims=True)
    return center * lax.rsqrt(spread + EPS) * gain + offset


def node_update(feats, scaled_agg, w_first, bias, w_second, w_third, gain, offset):
    joined = jnp.concatenate([feats, scaled_agg.astype(BF16)], axis=1)
    hidden = relu(jnp.dot(joined, w_first, preferred_element_type=F32) + bias)
    middle = relu(jnp.dot(hidden, w_second, preferred_element_type=F32))
    output = jnp.dot(middle, w_third, preferred_element_type=F32)
    return layer_norm(feats.astype(F32) + output, gain, offset).astype(BF16)


def order_rows(key_row, key_col, other_col, live_row, live_col, lanes, keys, starts, empty):
    slots = key_col.shape[0]
    iota = lambda shape, axis: lax.broadcasted_iota(jnp.int32, shape, axis)

    def by_group(key, values):
        out = values[0]
        for g in range(1, len(values)):
            out = jnp.where(key >= g * keys, values[g], out)
        return out

    floors = tuple(g * keys for g in range(len(starts)))
    lane = iota((slots, lanes), 1)
    before = (key_row == key_col) & (iota((slots, slots), 1) < iota((slots, slots), 0))
    within = jnp.sum(jnp.where(before, live_row, 0), axis=1, keepdims=True)
    counts = jnp.sum(jnp.where(lane == key_col, live_col, 0), axis=0, keepdims=True)
    counts_col = jnp.sum(jnp.where(iota((lanes, slots), 0) == key_row, live_row, 0), axis=1, keepdims=True)
    steps, steps_col = (counts + 1) >> 1, (counts_col + 1) >> 1
    chosen = (lane < key_col) & (lane >= by_group(key_col, floors))
    base_col = jnp.sum(jnp.where(chosen, steps, 0), axis=1, keepdims=True) + by_group(key_col, starts)
    place = jnp.where(live_col > 0, base_col * 2 + within, -1)
    hit = place == lane
    index = jnp.sum(jnp.where(hit, iota((slots, lanes), 0) - slots, 0), axis=0, keepdims=True) + slots
    other = jnp.sum(jnp.where(hit, other_col, 0), axis=0, keepdims=True)
    opens = (place == lane * 2) & (within == 0)
    carry = 1 - jnp.sum(jnp.where(opens, 1, 0), axis=0, keepdims=True)
    above, below = iota((lanes, lanes), 0), iota((1, lanes), 1)
    upto = (above <= below) & (above >= by_group(below, floors))
    ends = jnp.sum(jnp.where(upto, steps_col, 0), axis=0, keepdims=True) + by_group(below, starts)
    last = jnp.where(counts > 0, ends - 1, empty)
    rows = [index, other, carry, last]
    return jnp.concatenate(rows + [jnp.zeros((1, lanes), jnp.int32)] * (8 - len(rows)), axis=0)


def kernel(
    dims,
    cb_hbm, rb_hbm, count_s, vf_hbm, cf_hbm, coef_hbm,
    cw1_hbm, cbias_hbm, cw2_hbm, cw3_hbm, cgain_hbm, cshift_hbm,
    vw1_hbm, vbias_hbm, vw2_hbm, vw3_hbm, vgain_hbm, vshift_hbm,
    con_out, sums, base, feat, order_out, vw2, vw3, vgain, vshift,
    cb_v, rb_v, cf, cw1, cbias, cw2, cw3, cgain, cshift, vw1, vbias,
    raw, half, scan, paired, part, arrive, window, mixed, conbuf, orderf_v, orderf_s, orderb_v, orderb_s,
    raw_sem, feat_sem, small_sem, weight_sem, order_sem, psend, precv, wsend, wrecv, rsend,
):
    nb, nc, slots, size, cols, lanes, groups, steps, pairs = dims
    chunks = sum(groups)
    band = lax.axis_index("band")
    cut = lax.axis_index("cuts")
    has_next = band < nb - 1
    has_prev = band > 0
    width = feat.shape[2]
    cores = 2 if nc % 2 == 0 else 1
    chips = nc // cores
    chip, core = cut // cores, lax.rem(cut, cores)

    def member(far, which):
        return lax.rem(chip + far, chips) * cores + which

    far_first = [member(f, c) for f in range(chips - 1, 0, -1) for c in reversed(range(cores))]
    everyone = far_first + [member(0, c) for c in reversed(range(cores))]
    others = far_first + [member(0, cores - 1 - core)][: cores - 1]

    small = [
        pltpu.make_async_copy(src, dst, small_sem.at[i])
        for i, (src, dst) in enumerate(((cb_hbm, cb_v), (rb_hbm, rb_v)))
    ]
    for copy in small:
        copy.start()

    def raw_copy(i):
        piece = pl.ds(i * CHUNK, CHUNK)
        return pltpu.make_async_copy(coef_hbm.at[piece], raw.at[piece], raw_sem.at[i])

    for i in range(AHEAD):
        raw_copy(i).start()
    feat_copy = pltpu.make_async_copy(vf_hbm, feat, feat_sem)
    feat_copy.start()
    weights = [
        pltpu.make_async_copy(src, dst, weight_sem.at[i])
        for i, (src, dst) in enumerate((
            (cf_hbm, cf), (cw1_hbm, cw1), (cbias_hbm, cbias), (cw2_hbm, cw2), (cw3_hbm, cw3),
            (cgain_hbm, cgain), (cshift_hbm, cshift), (vw1_hbm, vw1), (vbias_hbm, vbias), (vw2_hbm, vw2),
            (vw3_hbm, vw3), (vgain_hbm, vgain), (vshift_hbm, vshift)))
    ]
    barrier = pltpu.get_barrier_semaphore()
    for d in range(1, nc):
        pl.semaphore_signal(barrier, inc=1, device_id=(band, lax.rem(cut + d, nc)), device_id_type=MESH)

    @pl.when(has_next)
    def _():
        for d in range(nc):
            pl.semaphore_signal(barrier, inc=1, device_id=(band + 1, lax.rem(cut + d, nc)), device_id_type=MESH)

    @pl.when(has_prev)
    def _():
        for d in range(nc):
            pl.semaphore_signal(barrier, inc=1, device_id=(band - 1, lax.rem(cut + d, nc)), device_id_type=MESH)

    half[slots] = jnp.zeros((size, size), BF16)
    scan[sum(steps)] = jnp.zeros((size, width), F32)
    sums[pairs] = jnp.zeros(sums.shape[1:], F32)

    @pl.when(jnp.logical_not(has_prev))
    def _():
        arrive[pl.ds(nc, nc)] = jnp.zeros((nc,) + arrive.shape[1:], BF16)

    @pl.when(jnp.logical_not(has_next))
    def _():
        window[pl.ds(nc, nc)] = jnp.zeros((nc,) + window.shape[1:], BF16)

    for copy in small:
        copy.wait()
    row_c = cb_v[...]
    row_r = rb_v[...]
    diagonal = lax.broadcasted_iota(jnp.int32, (slots, slots), 0) == lax.broadcasted_iota(jnp.int32, (slots, slots), 1)
    col_c = jnp.sum(jnp.where(diagonal, row_c, 0), axis=1, keepdims=True)
    col_r = jnp.sum(jnp.where(diagonal, row_r, 0), axis=1, keepdims=True)
    count = count_s[0]
    slot_row = lax.broadcasted_iota(jnp.int32, (1, slots), 1)
    slot_col = lax.broadcasted_iota(jnp.int32, (slots, 1), 0)
    live_row = jnp.where(slot_row < count, 1, 0)
    live_col = jnp.where(slot_col < count, 1, 0)
    blocks = part.shape[1] // size
    keys = 2 * nc * blocks
    bounds = [CHUNK * sum(groups[:g]) for g in range(1, len(groups))]
    starts = tuple(sum(steps[:g]) for g in range(len(groups)))
    late_row = sum(jnp.where(slot_row >= b, keys, 0) for b in bounds)
    late_col = sum(jnp.where(slot_col >= b, keys, 0) for b in bounds)
    orderf_v[...] = order_rows(
        row_r + late_row, col_r + late_col, col_c, live_row, live_col, lanes, keys, starts, sum(steps))
    orderf_copy = pltpu.make_async_copy(orderf_v, orderf_s, order_sem.at[0])
    orderf_copy.start()

    def convert(i):
        raw_copy(i).wait()

        @pl.when(i + AHEAD < chunks)
        def _():
            raw_copy(i + AHEAD).start()

        for u in range(CHUNK):
            half[i * CHUNK + u] = raw[i * CHUNK + u].astype(F32).astype(BF16)

    def convert_step(i, _):
        convert(i)
        return 0

    lax.fori_loop(0, groups[0], convert_step, 0)
    feat_copy.wait()
    orderf_copy.wait()

    carry = jnp.zeros((size, width), F32)
    for g, start in enumerate(starts):
        turns = groups[g + 1] if g + 1 < len(groups) else 1
        chunk = sum(groups[: g + 1])
        unroll = steps[g] // turns

        def forward(k, carry, start=start, unroll=unroll, chunk=chunk, more=g + 1 < len(groups)):
            for u in range(unroll):
                at = start + k * unroll + u
                left = jnp.concatenate([half[orderf_s[0, 2 * at]], half[orderf_s[0, 2 * at + 1]]], axis=1)
                right = jnp.concatenate(
                    [feat[orderf_s[1, 2 * at]], feat[orderf_s[1, 2 * at + 1]]], axis=0)
                term = jnp.dot(left, right, preferred_element_type=F32)
                carry = carry * orderf_s[2, at].astype(F32) + term
                scan[at] = carry
            if more:
                convert(chunk + k)
            return carry

        carry = lax.fori_loop(0, turns, forward, carry)
        if g == len(groups) - 2:
            for copy in weights:
                copy.start()

    def fill(q):
        for e in range(blocks):
            r = q * blocks + e
            total = scan[orderf_s[3, r]]
            for g in range(1, len(groups)):
                total += scan[orderf_s[3, g * keys + r]]
            part[q, e * size : (e + 1) * size] = total.astype(BF16)

    def part_send(i, to, ahead):
        return pltpu.make_async_remote_copy(
            src_ref=part.at[ahead * nc + to], dst_ref=arrive.at[ahead * nc + cut],
            send_sem=psend.at[ahead * nc + i], recv_sem=precv.at[ahead * nc + cut],
            device_id=(band + ahead, to), device_id_type=MESH)

    def part_wait(src, ahead):
        pltpu.make_async_remote_copy(
            src_ref=part.at[0], dst_ref=arrive.at[ahead * nc + src],
            send_sem=psend.at[0], recv_sem=precv.at[ahead * nc + src],
            device_id=(band, cut), device_id_type=MESH).wait_recv()

    for q in range(2 * nc):
        fill(q)

    expected = (nc - 1) + jnp.where(has_next, nc, 0) + jnp.where(has_prev, nc, 0)
    pl.semaphore_wait(barrier, expected)

    @pl.when(has_next)
    def _():
        for i, to in enumerate(everyone):
            part_send(i, to, 1).start()

    for i, to in enumerate(others):
        part_send(i, to, 0).start()

    orderb_v[...] = order_rows(row_c, col_c, col_r, live_row, live_col, lanes, lanes, (0,), pairs)
    orderb_copy = pltpu.make_async_copy(orderb_v, orderb_s, order_sem.at[1])
    orderb_copy.start()
    order_copy = pltpu.make_async_copy(orderb_v, order_out, order_sem.at[2])
    order_copy.start()
    for copy in weights:
        copy.wait()
    orderb_copy.wait()
    order_copy.wait()

    def pair_up(p, _):
        for u in range(PAIR):
            k = p * PAIR + u
            paired[k, :, :size] = half[orderb_s[0, 2 * k]].T
            paired[k, :, size:] = half[orderb_s[0, 2 * k + 1]].T
        return 0

    lax.fori_loop(0, pairs // PAIR, pair_up, 0)

    total = part[cut].astype(F32)
    for d in range(1, nc):
        src = lax.rem(cut + d, nc)
        part_wait(src, 0)
        total += arrive[src].astype(F32)

    @pl.when(has_prev)
    def _():
        for src in range(nc):
            part_wait(src, 1)

    for src in range(nc):
        total += arrive[nc + src].astype(F32)

    con_new = node_update(
        cf[...], total * (1.0 / math.sqrt(size * slots)), cw1[...], cbias[...], cw2[...], cw3[...], cgain[...], cshift[...])
    conbuf[...] = con_new
    window[cut] = con_new

    def win_send(i, to, back):
        return pltpu.make_async_remote_copy(
            src_ref=conbuf, dst_ref=window.at[back * nc + cut],
            send_sem=wsend.at[back * nc + i], recv_sem=wrecv.at[back * nc + cut],
            device_id=(band - back, to), device_id_type=MESH)

    def win_wait(src, back):
        pltpu.make_async_remote_copy(
            src_ref=conbuf, dst_ref=window.at[back * nc + src],
            send_sem=wsend.at[0], recv_sem=wrecv.at[back * nc + src],
            device_id=(band, cut), device_id_type=MESH).wait_recv()

    peer = member(0, cores - 1 - core)
    cross = [member(f, cores - 1 - core) for f in range(chips - 1, 0, -1)]
    rest = [member(f, core) for f in range(chips - 1, 0, -1)]
    ahead = cross + [peer]

    def relay(src, back):
        slot = back * nc + src
        return pltpu.make_async_remote_copy(
            src_ref=window.at[slot], dst_ref=window.at[slot],
            send_sem=rsend.at[slot], recv_sem=wrecv.at[slot],
            device_id=(band, peer), device_id_type=MESH)

    @pl.when(has_prev)
    def _():
        for i, to in enumerate(ahead):
            win_send(i, to, 1).start()

    for i, to in enumerate(cross + [peer]):
        win_send(i, to, 0).start()

    con_out[...] = con_new

    def base_step(i, _):
        for u in range(BASE):
            c = i * BASE + u
            base[c] = jnp.dot(feat[c], vw1[:width], preferred_element_type=F32) + vbias[...]
        return 0

    lax.fori_loop(0, cols // BASE, base_step, 0)

    def mix(q):
        for e in range(blocks):
            product = jnp.dot(window[q, e * size : (e + 1) * size], vw1[width:], preferred_element_type=F32)
            mixed[q * blocks + e] = (product * (1.0 / math.sqrt(4 * size))).astype(BF16)

    for src in cross:
        win_wait(src, 0)
        relay(src, 0).start()

    @pl.when(has_next)
    def _():
        for src in reversed(ahead):
            win_wait(src, 1)
            relay(src, 1).start()

    for src in [peer] + rest:
        win_wait(src, 0)
    for q in range(nc):
        mix(q)

    @pl.when(has_next)
    def _():
        for src in [cut] + rest:
            win_wait(src, 1)

    for q in range(nc, 2 * nc):
        mix(q)

    def back(k, carry):
        for u in range(BACK):
            at = k * BACK + u
            right = jnp.concatenate([mixed[orderb_s[1, 2 * at]], mixed[orderb_s[1, 2 * at + 1]]], axis=0)
            term = jnp.dot(paired[at], right, preferred_element_type=F32)
            carry = carry * orderb_s[2, at].astype(F32) + term
            sums[at] = carry
        return carry

    lax.fori_loop(0, pairs // BACK, back, jnp.zeros(sums.shape[1:], F32))

    @pl.when(has_next)
    def _():
        for i, to in enumerate(everyone):
            part_send(i, to, 1).wait_send()

    @pl.when(has_prev)
    def _():
        for i, to in enumerate(ahead):
            win_send(i, to, 1).wait_send()

    for i, to in enumerate(others):
        part_send(i, to, 0).wait_send()
    for i, to in enumerate(cross + [peer]):
        win_send(i, to, 0).wait_send()
    for src in cross:
        relay(src, 0).wait_send()

    @pl.when(has_next)
    def _():
        for src in ahead:
            relay(src, 1).wait_send()


def column_kernel(
    size, con, sums, base, feat, order_s, vw2, vw3, vgain, vshift, con_out, var_out,
    result, hidden, middle, output, out_sem, con_sem,
):
    con_copy = pltpu.make_async_copy(con, con_out, con_sem)
    con_copy.start()
    per = TILE // size
    tiles = feat.shape[0] // per
    piece = lambda i: pl.ds(i * TILE, TILE)

    def out_copy(i):
        return pltpu.make_async_copy(result.at[piece(i)], var_out.at[piece(i)], out_sem.at[i])

    def first(i):
        for e in range(per):
            c = i * per + e
            total = sums[order_s[3, c]] + base[c]
            hidden[i % 2, e * size : (e + 1) * size] = relu(total)

    def second(i):
        sums = jnp.dot(hidden[i % 2], vw2[...], preferred_element_type=F32)
        middle[i % 2] = relu(sums)

    def third(i):
        sums = jnp.dot(middle[i % 2], vw3[...], preferred_element_type=F32)
        output[i % 2] = feat[i * per : (i + 1) * per].reshape(sums.shape).astype(F32) + sums

    def norm(i):
        result[piece(i)] = layer_norm(output[i % 2], vgain[...], vshift[...]).astype(BF16)
        out_copy(i).start()

    stages = (norm, 3), (third, 2), (second, 1), (first, 0)
    for t in range(tiles + len(stages) - 1):
        for stage, delay in stages:
            if 0 <= t - delay < tiles:
                stage(t - delay)

    con_copy.wait()
    for i in range(tiles):
        out_copy(i).wait()


def on_device(
    nb, nc,
    var_feat, con_feat, slot_column_block, slot_constraint_block, block_count, incidence_coefficients,
    con_first, con_bias, con_second, con_third, con_gain, con_shift,
    var_first, var_bias, var_second, var_third, var_gain, var_shift,
):
    width = var_feat.shape[1]
    slots = slot_column_block.shape[0]
    size = incidence_coefficients.shape[1]
    cols = var_feat.shape[0] // size
    rows = con_feat.shape[0]
    rblocks = 2 * nc * (rows // size)
    chunks = slots // CHUNK
    tail = chunks // 5
    groups = (chunks - 2 * (chunks - tail) // 4 - tail, 2 * (chunks - tail) // 4, tail)
    turns = groups[1:] + (1,)
    steps = tuple(-(-(g * CHUNK + rblocks) // (2 * t)) * t for g, t in zip(groups, turns))
    pairs = -(-(slots + cols) // (2 * BACK)) * BACK
    lanes = -(-max(2 * pairs, 2 * sum(steps), 3 * rblocks) // 128) * 128
    dims = (nb, nc, slots, size, cols, lanes, groups, steps, pairs)
    vmem = pl.BlockSpec(memory_space=pltpu.VMEM)
    smem = pl.BlockSpec(memory_space=pltpu.SMEM)
    hbm = pl.BlockSpec(memory_space=pl.ANY)
    row = lambda v: v.reshape(1, -1)
    con_weights = (con_first, row(con_bias), con_second, con_third, row(con_gain), row(con_shift))
    var_weights = (var_first, row(var_bias), var_second, var_third, row(var_gain), row(var_shift))
    held = lambda v: pltpu.with_memory_space_constraint(v, pltpu.HBM)
    like = lambda v: pltpu.VMEM(v.shape, v.dtype)
    hid = var_first.shape[1]
    handed = pl.pallas_call(
        functools.partial(kernel, dims),
        out_shape=(
            like(con_feat),
            pltpu.VMEM((pairs + 1, size, hid), F32),
            pltpu.VMEM((cols, size, hid), F32),
            pltpu.VMEM((cols, size, width), BF16),
            pltpu.SMEM((8, lanes), jnp.int32),
            *(like(w) for w in var_weights[2:]),
        ),
        in_specs=[hbm] * 2 + [smem] + [hbm] * 15,
        out_specs=(vmem,) * 4 + (smem,) + (vmem,) * 4,
        scratch_shapes=[
            pltpu.VMEM((1, slots), jnp.int32),
            pltpu.VMEM((1, slots), jnp.int32),
            like(con_feat),
            *(like(w) for w in con_weights + var_weights[:2]),
            pltpu.VMEM((slots, size, size), jnp.int32),
            pltpu.VMEM((slots + 1, size, size), BF16),
            pltpu.VMEM((sum(steps) + 1, size, width), F32),
            pltpu.VMEM((pairs, size, 2 * size), BF16),
            pltpu.VMEM((2 * nc, rows, width), BF16),
            pltpu.VMEM((2 * nc, rows, width), BF16),
            pltpu.VMEM((2 * nc, rows, width), BF16),
            pltpu.VMEM((rblocks, size, hid), BF16),
            pltpu.VMEM((rows, width), BF16),
            pltpu.VMEM((8, lanes), jnp.int32),
            pltpu.SMEM((8, lanes), jnp.int32),
            pltpu.VMEM((8, lanes), jnp.int32),
            pltpu.SMEM((8, lanes), jnp.int32),
            pltpu.SemaphoreType.DMA((chunks,)),
            pltpu.SemaphoreType.DMA,
            pltpu.SemaphoreType.DMA((2,)),
            pltpu.SemaphoreType.DMA((13,)),
            pltpu.SemaphoreType.DMA((3,)),
            pltpu.SemaphoreType.DMA((2 * nc,)),
            pltpu.SemaphoreType.DMA((2 * nc,)),
            pltpu.SemaphoreType.DMA((2 * nc,)),
            pltpu.SemaphoreType.DMA((2 * nc,)),
            pltpu.SemaphoreType.DMA((2 * nc,)),
        ],
        compiler_params=pltpu.CompilerParams(
            collective_id=0, has_side_effects=True, vmem_limit_bytes=37 * 1024 * 1024),
        name="layer",
    )(
        *map(held, (row(slot_column_block), row(slot_constraint_block))), block_count,
        *map(held, (var_feat.reshape(cols, size, width), con_feat, incidence_coefficients, *con_weights, *var_weights)),
    )
    spaces = (pltpu.VMEM,) * 4 + (pltpu.SMEM,) + (pltpu.VMEM,) * 4
    return pl.pallas_call(
        functools.partial(column_kernel, size),
        out_shape=(
            jax.ShapeDtypeStruct(con_feat.shape, BF16),
            jax.ShapeDtypeStruct(var_feat.shape, BF16),
        ),
        in_specs=[vmem] * 4 + [smem] + [vmem] * 4,
        out_specs=(hbm, hbm),
        scratch_shapes=[
            pltpu.VMEM(var_feat.shape, BF16),
            pltpu.VMEM((2, TILE, hid), BF16),
            pltpu.VMEM((2, TILE, var_second.shape[1]), BF16),
            pltpu.VMEM((2, TILE, width), F32),
            pltpu.SemaphoreType.DMA((var_feat.shape[0] // TILE,)),
            pltpu.SemaphoreType.DMA,
        ],
        compiler_params=pltpu.CompilerParams(vmem_limit_bytes=8 * 1024 * 1024),
        name="columns",
    )(*map(pltpu.with_memory_space_constraint, handed, spaces))


def solution(mesh):
    both = P(("band", "cuts"))
    wide = P(("band", "cuts"), None)
    in_specs = (wide, wide, both, both, both, P(("band", "cuts"), None, None)) + (P(),) * 12
    body = functools.partial(on_device, mesh.shape["band"], mesh.shape["cuts"])
    return jax.shard_map(body, mesh=mesh, in_specs=in_specs, out_specs=(wide, wide), check_vma=False)
```

```python
import functools
import math

import jax
import jax.numpy as jnp
from jax import lax
from jax.experimental import pallas as pl
from jax.experimental.pallas import tpu as pltpu
from jax.sharding import PartitionSpec as P

EPS = 1e-05
F32 = jnp.float32
BF16 = jnp.bfloat16
MESH = pl.DeviceIdType.MESH
CHUNK = 16
UNROLL = 8
BACK = 100
PAIR = 5
BASE = 4
AHEAD = 4
TILE = 512


def relu(values):
    return jnp.maximum(values.astype(BF16), jnp.zeros((), BF16))


def layer_norm(values, gain, offset):
    center = values - jnp.mean(values, axis=-1, keepdims=True)
    spread = jnp.mean(center * center, axis=-1, keepdims=True)
    return center * lax.rsqrt(spread + EPS) * gain + offset


def node_update(feats, scaled_agg, w_first, bias, w_second, w_third, gain, offset):
    joined = jnp.concatenate([feats, scaled_agg.astype(BF16)], axis=1)
    hidden = relu(jnp.dot(joined, w_first, preferred_element_type=F32) + bias)
    middle = relu(jnp.dot(hidden, w_second, preferred_element_type=F32))
    output = jnp.dot(middle, w_third, preferred_element_type=F32)
    return layer_norm(feats.astype(F32) + output, gain, offset).astype(BF16)


def order_rows(key_row, key_col, other_col, live_row, live_col, lanes, keys, starts, empty):
    slots = key_col.shape[0]
    iota = lambda shape, axis: lax.broadcasted_iota(jnp.int32, shape, axis)

    def by_group(key, values):
        out = values[0]
        for g in range(1, len(values)):
            out = jnp.where(key >= g * keys, values[g], out)
        return out

    floors = tuple(g * keys for g in range(len(starts)))
    lane = iota((slots, lanes), 1)
    before = (key_row == key_col) & (iota((slots, slots), 1) < iota((slots, slots), 0))
    within = jnp.sum(jnp.where(before, live_row, 0), axis=1, keepdims=True)
    counts = jnp.sum(jnp.where(lane == key_col, live_col, 0), axis=0, keepdims=True)
    counts_col = jnp.sum(jnp.where(iota((lanes, slots), 0) == key_row, live_row, 0), axis=1, keepdims=True)
    steps, steps_col = (counts + 1) >> 1, (counts_col + 1) >> 1
    chosen = (lane < key_col) & (lane >= by_group(key_col, floors))
    base_col = jnp.sum(jnp.where(chosen, steps, 0), axis=1, keepdims=True) + by_group(key_col, starts)
    place = jnp.where(live_col > 0, base_col * 2 + within, -1)
    hit = place == lane
    index = jnp.sum(jnp.where(hit, iota((slots, lanes), 0) - slots, 0), axis=0, keepdims=True) + slots
    other = jnp.sum(jnp.where(hit, other_col, 0), axis=0, keepdims=True)
    opens = (place == lane * 2) & (within == 0)
    carry = 1 - jnp.sum(jnp.where(opens, 1, 0), axis=0, keepdims=True)
    above, below = iota((lanes, lanes), 0), iota((1, lanes), 1)
    upto = (above <= below) & (above >= by_group(below, floors))
    ends = jnp.sum(jnp.where(upto, steps_col, 0), axis=0, keepdims=True) + by_group(below, starts)
    last = jnp.where(counts > 0, ends - 1, empty)
    rows = [index, other, carry, last]
    return jnp.concatenate(rows + [jnp.zeros((1, lanes), jnp.int32)] * (8 - len(rows)), axis=0)


def kernel(
    dims,
    cb_hbm, rb_hbm, count_s, vf_hbm, cf_hbm, coef_hbm,
    cw1_hbm, cbias_hbm, cw2_hbm, cw3_hbm, cgain_hbm, cshift_hbm,
    vw1_hbm, vbias_hbm, vw2_hbm, vw3_hbm, vgain_hbm, vshift_hbm,
    con_out, sums, base, feat, order_out, vw2, vw3, vgain, vshift,
    cb_v, rb_v, cf, cw1, cbias, cw2, cw3, cgain, cshift, vw1, vbias,
    raw, half, scan, paired, part, arrive, window, mixed, conbuf, orderf_v, orderf_s, orderb_v, orderb_s,
    raw_sem, feat_sem, small_sem, weight_sem, order_sem, psend, precv, wsend, wrecv, rsend,
):
    nb, nc, slots, size, cols, lanes, groups, steps, pairs = dims
    chunks = sum(groups)
    band = lax.axis_index("band")
    cut = lax.axis_index("cuts")
    has_next = band < nb - 1
    has_prev = band > 0
    width = feat.shape[2]
    cores = 2 if nc % 2 == 0 else 1
    chips = nc // cores
    chip, core = cut // cores, lax.rem(cut, cores)

    def member(far, which):
        return lax.rem(chip + far, chips) * cores + which

    far_first = [member(f, c) for f in range(chips - 1, 0, -1) for c in reversed(range(cores))]
    everyone = far_first + [member(0, c) for c in reversed(range(cores))]
    others = far_first + [member(0, cores - 1 - core)][: cores - 1]

    small = [
        pltpu.make_async_copy(src, dst, small_sem.at[i])
        for i, (src, dst) in enumerate(((cb_hbm, cb_v), (rb_hbm, rb_v)))
    ]
    for copy in small:
        copy.start()

    def raw_copy(i):
        piece = pl.ds(i * CHUNK, CHUNK)
        return pltpu.make_async_copy(coef_hbm.at[piece], raw.at[piece], raw_sem.at[i])

    for i in range(AHEAD):
        raw_copy(i).start()
    feat_copy = pltpu.make_async_copy(vf_hbm, feat, feat_sem)
    feat_copy.start()
    weights = [
        pltpu.make_async_copy(src, dst, weight_sem.at[i])
        for i, (src, dst) in enumerate((
            (cf_hbm, cf), (cw1_hbm, cw1), (cbias_hbm, cbias), (cw2_hbm, cw2), (cw3_hbm, cw3),
            (cgain_hbm, cgain), (cshift_hbm, cshift), (vw1_hbm, vw1), (vbias_hbm, vbias), (vw2_hbm, vw2),
            (vw3_hbm, vw3), (vgain_hbm, vgain), (vshift_hbm, vshift)))
    ]
    barrier = pltpu.get_barrier_semaphore()
    for d in range(1, nc):
        pl.semaphore_signal(barrier, inc=1, device_id=(band, lax.rem(cut + d, nc)), device_id_type=MESH)

    @pl.when(has_next)
    def _():
        for d in range(nc):
            pl.semaphore_signal(barrier, inc=1, device_id=(band + 1, lax.rem(cut + d, nc)), device_id_type=MESH)

    @pl.when(has_prev)
    def _():
        for d in range(nc):
            pl.semaphore_signal(barrier, inc=1, device_id=(band - 1, lax.rem(cut + d, nc)), device_id_type=MESH)

    half[slots] = jnp.zeros((size, size), BF16)
    scan[sum(steps)] = jnp.zeros((size, width), F32)
    sums[pairs] = jnp.zeros(sums.shape[1:], F32)

    @pl.when(jnp.logical_not(has_prev))
    def _():
        arrive[pl.ds(nc, nc)] = jnp.zeros((nc,) + arrive.shape[1:], BF16)

    @pl.when(jnp.logical_not(has_next))
    def _():
        window[pl.ds(nc, nc)] = jnp.zeros((nc,) + window.shape[1:], BF16)

    for copy in small:
        copy.wait()
    row_c = cb_v[...]
    row_r = rb_v[...]
    diagonal = lax.broadcasted_iota(jnp.int32, (slots, slots), 0) == lax.broadcasted_iota(jnp.int32, (slots, slots), 1)
    col_c = jnp.sum(jnp.where(diagonal, row_c, 0), axis=1, keepdims=True)
    col_r = jnp.sum(jnp.where(diagonal, row_r, 0), axis=1, keepdims=True)
    count = count_s[0]
    slot_row = lax.broadcasted_iota(jnp.int32, (1, slots), 1)
    slot_col = lax.broadcasted_iota(jnp.int32, (slots, 1), 0)
    live_row = jnp.where(slot_row < count, 1, 0)
    live_col = jnp.where(slot_col < count, 1, 0)
    blocks = part.shape[1] // size
    keys = 2 * nc * blocks
    bounds = [CHUNK * sum(groups[:g]) for g in range(1, len(groups))]
    starts = tuple(sum(steps[:g]) for g in range(len(groups)))
    late_row = sum(jnp.where(slot_row >= b, keys, 0) for b in bounds)
    late_col = sum(jnp.where(slot_col >= b, keys, 0) for b in bounds)
    orderf_v[...] = order_rows(
        row_r + late_row, col_r + late_col, col_c, live_row, live_col, lanes, keys, starts, sum(steps))
    orderf_copy = pltpu.make_async_copy(orderf_v, orderf_s, order_sem.at[0])
    orderf_copy.start()

    def convert(i):
        raw_copy(i).wait()

        @pl.when(i + AHEAD < chunks)
        def _():
            raw_copy(i + AHEAD).start()

        for u in range(CHUNK):
            half[i * CHUNK + u] = raw[i * CHUNK + u].astype(F32).astype(BF16)

    def convert_step(i, _):
        convert(i)
        return 0

    lax.fori_loop(0, groups[0], convert_step, 0)
    feat_copy.wait()
    orderf_copy.wait()

    carry = jnp.zeros((size, width), F32)
    for g, start in enumerate(starts):
        turns = groups[g + 1] if g + 1 < len(groups) else 1
        chunk = sum(groups[: g + 1])
        unroll = steps[g] // turns

        def forward(k, carry, start=start, unroll=unroll, chunk=chunk, more=g + 1 < len(groups)):
            for u in range(unroll):
                at = start + k * unroll + u
                left = jnp.concatenate([half[orderf_s[0, 2 * at]], half[orderf_s[0, 2 * at + 1]]], axis=1)
                right = jnp.concatenate(
                    [feat[orderf_s[1, 2 * at]], feat[orderf_s[1, 2 * at + 1]]], axis=0)
                term = jnp.dot(left, right, preferred_element_type=F32)
                carry = carry * orderf_s[2, at].astype(F32) + term
                scan[at] = carry
            if more:
                convert(chunk + k)
            return carry

        carry = lax.fori_loop(0, turns, forward, carry)
        if g == len(groups) - 2:
            for copy in weights:
                copy.start()

    def fill(q):
        for e in range(blocks):
            r = q * blocks + e
            total = scan[orderf_s[3, r]]
            for g in range(1, len(groups)):
                total += scan[orderf_s[3, g * keys + r]]
            part[q, e * size : (e + 1) * size] = total.astype(BF16)

    def part_send(i, to, ahead):
        return pltpu.make_async_remote_copy(
            src_ref=part.at[ahead * nc + to], dst_ref=arrive.at[ahead * nc + cut],
            send_sem=psend.at[ahead * nc + i], recv_sem=precv.at[ahead * nc + cut],
            device_id=(band + ahead, to), device_id_type=MESH)

    def part_wait(src, ahead):
        pltpu.make_async_remote_copy(
            src_ref=part.at[0], dst_ref=arrive.at[ahead * nc + src],
            send_sem=psend.at[0], recv_sem=precv.at[ahead * nc + src],
            device_id=(band, cut), device_id_type=MESH).wait_recv()

    for q in range(2 * nc):
        fill(q)

    expected = (nc - 1) + jnp.where(has_next, nc, 0) + jnp.where(has_prev, nc, 0)
    pl.semaphore_wait(barrier, expected)

    @pl.when(has_next)
    def _():
        for i, to in enumerate(everyone):
            part_send(i, to, 1).start()

    for i, to in enumerate(others):
        part_send(i, to, 0).start()

    orderb_v[...] = order_rows(row_c, col_c, col_r, live_row, live_col, lanes, lanes, (0,), pairs)
    orderb_copy = pltpu.make_async_copy(orderb_v, orderb_s, order_sem.at[1])
    orderb_copy.start()
    order_copy = pltpu.make_async_copy(orderb_v, order_out, order_sem.at[2])
    order_copy.start()
    for copy in weights:
        copy.wait()
    orderb_copy.wait()
    order_copy.wait()

    def pair_up(p, _):
        for u in range(PAIR):
            k = p * PAIR + u
            paired[k, :, :size] = half[orderb_s[0, 2 * k]].T
            paired[k, :, size:] = half[orderb_s[0, 2 * k + 1]].T
        return 0

    lax.fori_loop(0, pairs // PAIR, pair_up, 0)

    total = part[cut].astype(F32)
    for d in range(1, nc):
        src = lax.rem(cut + d, nc)
        part_wait(src, 0)
        total += arrive[src].astype(F32)

    @pl.when(has_prev)
    def _():
        for src in range(nc):
            part_wait(src, 1)

    for src in range(nc):
        total += arrive[nc + src].astype(F32)

    con_new = node_update(
        cf[...], total * (1.0 / math.sqrt(size * slots)), cw1[...], cbias[...], cw2[...], cw3[...], cgain[...], cshift[...])
    conbuf[...] = con_new
    window[cut] = con_new

    def win_send(i, to, back):
        return pltpu.make_async_remote_copy(
            src_ref=conbuf, dst_ref=window.at[back * nc + cut],
            send_sem=wsend.at[back * nc + i], recv_sem=wrecv.at[back * nc + cut],
            device_id=(band - back, to), device_id_type=MESH)

    def win_wait(src, back):
        pltpu.make_async_remote_copy(
            src_ref=conbuf, dst_ref=window.at[back * nc + src],
            send_sem=wsend.at[0], recv_sem=wrecv.at[back * nc + src],
            device_id=(band, cut), device_id_type=MESH).wait_recv()

    peer = member(0, cores - 1 - core)
    cross = [member(f, cores - 1 - core) for f in range(chips - 1, 0, -1)]
    rest = [member(f, core) for f in range(chips - 1, 0, -1)]
    ahead = cross + [peer]

    def relay(src, back):
        slot = back * nc + src
        return pltpu.make_async_remote_copy(
            src_ref=window.at[slot], dst_ref=window.at[slot],
            send_sem=rsend.at[slot], recv_sem=wrecv.at[slot],
            device_id=(band, peer), device_id_type=MESH)

    @pl.when(has_prev)
    def _():
        for i, to in enumerate(ahead):
            win_send(i, to, 1).start()

    for i, to in enumerate(cross + [peer]):
        win_send(i, to, 0).start()

    con_out[...] = con_new

    def base_step(i, _):
        for u in range(BASE):
            c = i * BASE + u
            base[c] = jnp.dot(feat[c], vw1[:width], preferred_element_type=F32) + vbias[...]
        return 0

    lax.fori_loop(0, cols // BASE, base_step, 0)

    def mix(q):
        for e in range(blocks):
            product = jnp.dot(window[q, e * size : (e + 1) * size], vw1[width:], preferred_element_type=F32)
            mixed[q * blocks + e] = (product * (1.0 / math.sqrt(4 * size))).astype(BF16)

    for src in cross:
        win_wait(src, 0)
        relay(src, 0).start()

    @pl.when(has_next)
    def _():
        for src in reversed(ahead):
            win_wait(src, 1)
            relay(src, 1).start()

    @pl.when(has_next)
    def _():
        for i, to in enumerate(everyone):
            part_send(i, to, 1).wait_send()

    @pl.when(has_prev)
    def _():
        for i, to in enumerate(ahead):
            win_send(i, to, 1).wait_send()

    for i, to in enumerate(others):
        part_send(i, to, 0).wait_send()
    for i, to in enumerate(cross + [peer]):
        win_send(i, to, 0).wait_send()

    for src in [peer] + rest:
        win_wait(src, 0)
    for q in range(nc):
        mix(q)

    @pl.when(has_next)
    def _():
        for src in [cut] + rest:
            win_wait(src, 1)

    for q in range(nc, 2 * nc):
        mix(q)

    def back(k, carry):
        for u in range(BACK):
            at = k * BACK + u
            right = jnp.concatenate([mixed[orderb_s[1, 2 * at]], mixed[orderb_s[1, 2 * at + 1]]], axis=0)
            term = jnp.dot(paired[at], right, preferred_element_type=F32)
            carry = carry * orderb_s[2, at].astype(F32) + term
            sums[at] = carry
        return carry

    lax.fori_loop(0, pairs // BACK, back, jnp.zeros(sums.shape[1:], F32))

    for src in cross:
        relay(src, 0).wait_send()

    @pl.when(has_next)
    def _():
        for src in ahead:
            relay(src, 1).wait_send()


def column_kernel(
    size, con, sums, base, feat, order_s, vw2, vw3, vgain, vshift, con_out, var_out,
    result, hidden, middle, output, out_sem, con_sem,
):
    con_copy = pltpu.make_async_copy(con, con_out, con_sem)
    con_copy.start()
    per = TILE // size
    tiles = feat.shape[0] // per
    piece = lambda i: pl.ds(i * TILE, TILE)

    def out_copy(i):
        return pltpu.make_async_copy(result.at[piece(i)], var_out.at[piece(i)], out_sem.at[i])

    def first(i):
        for e in range(per):
            c = i * per + e
            total = sums[order_s[3, c]] + base[c]
            hidden[i % 2, e * size : (e + 1) * size] = relu(total)

    def second(i):
        sums = jnp.dot(hidden[i % 2], vw2[...], preferred_element_type=F32)
        middle[i % 2] = relu(sums)

    def third(i):
        sums = jnp.dot(middle[i % 2], vw3[...], preferred_element_type=F32)
        output[i % 2] = feat[i * per : (i + 1) * per].reshape(sums.shape).astype(F32) + sums

    def norm(i):
        result[piece(i)] = layer_norm(output[i % 2], vgain[...], vshift[...]).astype(BF16)
        out_copy(i).start()

    stages = (norm, 3), (third, 2), (second, 1), (first, 0)
    for t in range(tiles + len(stages) - 1):
        for stage, delay in stages:
            if 0 <= t - delay < tiles:
                stage(t - delay)

    con_copy.wait()
    for i in range(tiles):
        out_copy(i).wait()


def on_device(
    nb, nc,
    var_feat, con_feat, slot_column_block, slot_constraint_block, block_count, incidence_coefficients,
    con_first, con_bias, con_second, con_third, con_gain, con_shift,
    var_first, var_bias, var_second, var_third, var_gain, var_shift,
):
    width = var_feat.shape[1]
    slots = slot_column_block.shape[0]
    size = incidence_coefficients.shape[1]
    cols = var_feat.shape[0] // size
    rows = con_feat.shape[0]
    rblocks = 2 * nc * (rows // size)
    chunks = slots // CHUNK
    tail = chunks // 5
    groups = (chunks - 2 * (chunks - tail) // 4 - tail, 2 * (chunks - tail) // 4, tail)
    turns = groups[1:] + (1,)
    steps = tuple(-(-(g * CHUNK + rblocks) // (2 * t)) * t for g, t in zip(groups, turns))
    pairs = -(-(slots + cols) // (2 * BACK)) * BACK
    lanes = -(-max(2 * pairs, 2 * sum(steps), 3 * rblocks) // 128) * 128
    dims = (nb, nc, slots, size, cols, lanes, groups, steps, pairs)
    vmem = pl.BlockSpec(memory_space=pltpu.VMEM)
    smem = pl.BlockSpec(memory_space=pltpu.SMEM)
    hbm = pl.BlockSpec(memory_space=pl.ANY)
    row = lambda v: v.reshape(1, -1)
    con_weights = (con_first, row(con_bias), con_second, con_third, row(con_gain), row(con_shift))
    var_weights = (var_first, row(var_bias), var_second, var_third, row(var_gain), row(var_shift))
    held = lambda v: pltpu.with_memory_space_constraint(v, pltpu.HBM)
    like = lambda v: pltpu.VMEM(v.shape, v.dtype)
    hid = var_first.shape[1]
    handed = pl.pallas_call(
        functools.partial(kernel, dims),
        out_shape=(
            like(con_feat),
            pltpu.VMEM((pairs + 1, size, hid), F32),
            pltpu.VMEM((cols, size, hid), F32),
            pltpu.VMEM((cols, size, width), BF16),
            pltpu.SMEM((8, lanes), jnp.int32),
            *(like(w) for w in var_weights[2:]),
        ),
        in_specs=[hbm] * 2 + [smem] + [hbm] * 15,
        out_specs=(vmem,) * 4 + (smem,) + (vmem,) * 4,
        scratch_shapes=[
            pltpu.VMEM((1, slots), jnp.int32),
            pltpu.VMEM((1, slots), jnp.int32),
            like(con_feat),
            *(like(w) for w in con_weights + var_weights[:2]),
            pltpu.VMEM((slots, size, size), jnp.int32),
            pltpu.VMEM((slots + 1, size, size), BF16),
            pltpu.VMEM((sum(steps) + 1, size, width), F32),
            pltpu.VMEM((pairs, size, 2 * size), BF16),
            pltpu.VMEM((2 * nc, rows, width), BF16),
            pltpu.VMEM((2 * nc, rows, width), BF16),
            pltpu.VMEM((2 * nc, rows, width), BF16),
            pltpu.VMEM((rblocks, size, hid), BF16),
            pltpu.VMEM((rows, width), BF16),
            pltpu.VMEM((8, lanes), jnp.int32),
            pltpu.SMEM((8, lanes), jnp.int32),
            pltpu.VMEM((8, lanes), jnp.int32),
            pltpu.SMEM((8, lanes), jnp.int32),
            pltpu.SemaphoreType.DMA((chunks,)),
            pltpu.SemaphoreType.DMA,
            pltpu.SemaphoreType.DMA((2,)),
            pltpu.SemaphoreType.DMA((13,)),
            pltpu.SemaphoreType.DMA((3,)),
            pltpu.SemaphoreType.DMA((2 * nc,)),
            pltpu.SemaphoreType.DMA((2 * nc,)),
            pltpu.SemaphoreType.DMA((2 * nc,)),
            pltpu.SemaphoreType.DMA((2 * nc,)),
            pltpu.SemaphoreType.DMA((2 * nc,)),
        ],
        compiler_params=pltpu.CompilerParams(
            collective_id=0, has_side_effects=True, vmem_limit_bytes=37 * 1024 * 1024),
        name="layer",
    )(
        *map(held, (row(slot_column_block), row(slot_constraint_block))), block_count,
        *map(held, (var_feat.reshape(cols, size, width), con_feat, incidence_coefficients, *con_weights, *var_weights)),
    )
    spaces = (pltpu.VMEM,) * 4 + (pltpu.SMEM,) + (pltpu.VMEM,) * 4
    return pl.pallas_call(
        functools.partial(column_kernel, size),
        out_shape=(
            jax.ShapeDtypeStruct(con_feat.shape, BF16),
            jax.ShapeDtypeStruct(var_feat.shape, BF16),
        ),
        in_specs=[vmem] * 4 + [smem] + [vmem] * 4,
        out_specs=(hbm, hbm),
        scratch_shapes=[
            pltpu.VMEM(var_feat.shape, BF16),
            pltpu.VMEM((2, TILE, hid), BF16),
            pltpu.VMEM((2, TILE, var_second.shape[1]), BF16),
            pltpu.VMEM((2, TILE, width), F32),
            pltpu.SemaphoreType.DMA((var_feat.shape[0] // TILE,)),
            pltpu.SemaphoreType.DMA,
        ],
        compiler_params=pltpu.CompilerParams(vmem_limit_bytes=8 * 1024 * 1024),
        name="columns",
    )(*map(pltpu.with_memory_space_constraint, handed, spaces))


def solution(mesh):
    both = P(("band", "cuts"))
    wide = P(("band", "cuts"), None)
    in_specs = (wide, wide, both, both, both, P(("band", "cuts"), None, None)) + (P(),) * 12
    body = functools.partial(on_device, mesh.shape["band"], mesh.shape["cuts"])
    return jax.shard_map(body, mesh=mesh, in_specs=in_specs, out_specs=(wide, wide), check_vma=False)
```
